32 devices in a mesh: rect: 4 (over y, x), slab: 8 (over z, core).
Axes of the slice: x: 2, y: 2, z: 4, core: 2. Of those that a mesh axis runs over, the one named last changes fastest.
Arguments:
- modes_now: bfloat16 [4, 512, 256, 256], P('rect', None, 'slab'), may hold values from -4 to 4
- modes_prev: bfloat16 [4, 512, 256, 256], P('rect', None, 'slab'), may hold values from -4 to 4
- face_partner: int32 [4], replicated, may hold values from 0 to 3, each once
Outputs:
- modes_next: bfloat16 [4, 512, 256, 256], P('rect', None, 'slab')
- interface_force: float32 [4, 6, 512, 256], P('rect', None, 'slab')
The draws below stay inside these ranges and needn't reach their ends.
Inputs may be any that keep to these rules, and one draw needn't show every extreme that they name: `face_partner`: A permutation of the large rectangles; a rectangle may abut itself.
All inputs are finite; a program needn't handle non-finite values.
Results may differ from the reference program's by a relative error of at most 0.0048.
The reference program's roundings to bfloat16 on the way count: a program that leaves them out, or rounds other values in their place, can miss the bound.
Values may be sent and summed in bfloat16 or wider, within the bound.
No kernel may reach another device: no remote copies, remote signals or barrier semaphores. Data moves between devices by JAX's collectives and lax.ppermute only.
A program may use at most 64 MiB of HBM per device.

```python
import math
import jax
import jax.numpy as jnp
from jax import lax

X = 512
Y = 256
Z = 256
RECTS = 4


def levels(stream_key, dims, shards, low, top_value):
    loudness = 1.0
    for axis_at, shards_of in shards:
        heights = jax.random.uniform(jax.random.fold_in(jax.random.fold_in(stream_key, 6), axis_at), (shards_of,), jnp.float32, low / len(shards), top_value / len(shards))
        loudness = loudness * jnp.repeat(jnp.exp(heights), dims[axis_at] // shards_of).reshape((-1,) + (1,) * (len(dims) - 1 - axis_at))
    return loudness


def gaussian(key, shape, scale, limit, split=(), held_as=jnp.bfloat16):
    values = scale * jax.random.normal(key, shape, jnp.float32)
    if split:
        values = values * levels(key, shape, split, -0.22, 0.18)
    return jnp.clip(values, -limit, limit).astype(held_as)


def setup_inputs(seed: int = 0) -> dict:
    streams_of = jax.random.split(jax.random.key(seed), 4)
    return {
        "modes_now": gaussian(streams_of[0], (RECTS, X, Y, Z), 1.0, 4.0, ((0, 4), (2, 8))),
        "modes_prev": gaussian(streams_of[1], (RECTS, X, Y, Z), 1.0, 4.0, ((0, 4), (2, 8))),
        "face_partner": jax.random.permutation(streams_of[2], RECTS).astype(jnp.int32),
    }


courant_sq = 1.0 / 3.0
coeffs = (1.5, -0.15, 2.0 / 180.0)
theta_scale = math.pi / math.sqrt(3.0)

def cosine_table(length):
    mode_index = jnp.arange(length, dtype=jnp.int32)[:, None]
    cell_index = jnp.arange(length, dtype=jnp.int32)[None, :]
    phase_turns = mode_index * (2 * cell_index + 1) % (4 * length)
    angles = phase_turns.astype(jnp.float32) * (math.pi / (2.0 * length))
    weights = jnp.where(mode_index == 0, math.sqrt(1.0 / length), math.sqrt(2.0 / length)).astype(jnp.float32)
    return weights * jnp.cos(angles)

def face_columns(table, depth_z):
    return jnp.concatenate([table[:, :3], table[:, depth_z - 3:]], axis=1)

def box_theta(first_modes, second_modes, third_modes, sides):
    first_part = first_modes.astype(jnp.float32) / sides[0]
    second_part = second_modes.astype(jnp.float32) / sides[1]
    third_part = third_modes.astype(jnp.float32) / sides[2]
    summed = (first_part * first_part)[:, None, None] + (second_part * second_part)[None, :, None] + (third_part * third_part)[None, None, :]
    return theta_scale * jnp.sqrt(summed)

def modal_factors(theta):
    positive = theta > 0.0
    safe_theta = jnp.where(positive, theta, 1.0)
    ratio_term = 2.0 * jnp.sin(0.5 * safe_theta) / safe_theta
    return (2.0 * jnp.cos(theta), jnp.where(positive, ratio_term * ratio_term, 1.0))

def face_force(lower, upper, partner_lower, source_upper):
    jump_up = [partner_lower[offset] - upper[2 - offset] for offset in range(3)]
    jump_down = [source_upper[2 - offset] - lower[offset] for offset in range(3)]
    lower_force = []
    upper_force = []
    for plane_rank in range(3):
        lower_sum = coeffs[plane_rank] * jump_down[0]
        upper_sum = coeffs[plane_rank] * jump_up[0]
        for offset in range(1, 3 - plane_rank):
            lower_sum = lower_sum + coeffs[plane_rank + offset] * jump_down[offset]
            upper_sum = upper_sum + coeffs[plane_rank + offset] * jump_up[offset]
        lower_force.append(courant_sq * lower_sum)
        upper_force.append(courant_sq * upper_sum)
    return jnp.stack(lower_force + upper_force[::-1], axis=0)

def widen(array):
    return array.astype(jnp.float32)

def reference(modes_now, modes_prev, face_partner):
    table_x = cosine_table(X).astype(jnp.bfloat16)
    table_y = cosine_table(Y).astype(jnp.bfloat16)
    plane_cols = face_columns(cosine_table(Z), Z).astype(jnp.bfloat16)

    def inverse(modes):
        section_z = jnp.einsum('xyk,kp->pxy', widen(modes), widen(plane_cols)).astype(jnp.bfloat16)
        section_x = jnp.einsum('kn,pky->pny', widen(table_x), widen(section_z)).astype(jnp.bfloat16)
        return jnp.einsum('pxk,kn->pxn', widen(section_x), widen(table_y))
    planes = lax.map(inverse, modes_now)
    rect_ids = jnp.arange(RECTS, dtype=jnp.int32)
    source_ids = jnp.zeros((RECTS,), jnp.int32).at[face_partner].set(rect_ids)
    partner_lower = planes[face_partner, :3]
    source_upper = planes[source_ids, 3:]
    forcing = jax.vmap(face_force)(planes[:, :3], planes[:, 3:], partner_lower, source_upper)
    theta = box_theta(jnp.arange(X, dtype=jnp.int32), jnp.arange(Y, dtype=jnp.int32), jnp.arange(Z, dtype=jnp.int32), (X, Y, Z))
    two_cos, gain_table = modal_factors(theta)

    def advance(packed):
        now_part, prev_part, force_part = packed
        force_half = force_part.astype(jnp.bfloat16)
        spec_y = jnp.einsum('pxn,kn->pxk', widen(force_half), widen(table_y)).astype(jnp.bfloat16)
        spec_x = jnp.einsum('kn,pny->pky', widen(table_x), widen(spec_y)).astype(jnp.bfloat16)
        modal_force = jnp.einsum('pxy,kp->xyk', widen(spec_x), widen(plane_cols))
        return (two_cos * widen(now_part) - widen(prev_part) + gain_table * modal_force).astype(jnp.bfloat16)
    modes_next = lax.map(advance, (modes_now, modes_prev, forcing))
    return (modes_next, forcing)
```

```python
import functools
import math

import jax
import jax.numpy as jnp
import ml_dtypes
import numpy as np
from jax import lax
from jax.experimental import pallas as pl
from jax.experimental.pallas import tpu as pltpu
from jax.sharding import PartitionSpec as P

courant_sq = 1.0 / 3.0
coeffs = (1.5, -0.15, 2.0 / 180.0)
bf16 = ml_dtypes.bfloat16
PLANES = 6
LANES = 128
GROUP = 16
USED = PLANES * GROUP


def cosine_table(length):
    mode_index = np.arange(length, dtype=np.int64)[:, None]
    cell_index = np.arange(length, dtype=np.int64)[None, :]
    phase = mode_index * (2 * cell_index + 1) % (4 * length)
    angles = phase.astype(np.float32) * np.float32(math.pi / (2.0 * length))
    weights = np.where(mode_index == 0, math.sqrt(1.0 / length), math.sqrt(2.0 / length))
    return weights.astype(np.float32) * np.cos(angles)


def plane_columns(depth_z):
    table = cosine_table(depth_z)
    return np.concatenate([table[:, :3], table[:, depth_z - 3 :]], axis=1).astype(bf16)


def spread_columns(depth_z):
    columns = plane_columns(depth_z)
    out = np.zeros((depth_z, LANES), bf16)
    out[:, :USED] = np.repeat(columns, GROUP, axis=1)
    return out


def force_matrix():
    own = np.zeros((PLANES, PLANES), np.float64)
    other = np.zeros((PLANES, PLANES), np.float64)
    for m in range(3):
        for k in range(3 - m):
            weight = courant_sq * coeffs[m + k]
            other[5 - k, m] += weight
            own[k, m] -= weight
            other[k, 5 - m] += weight
            own[5 - k, 5 - m] -= weight
    full = np.zeros((2 * LANES, LANES), np.float64)
    for row in range(GROUP):
        full[row:USED:GROUP, row:USED:GROUP] = own
        full[LANES + row : LANES + USED : GROUP, row:USED:GROUP] = other
    terms = []
    rest = full
    for _ in range(3):
        term = rest.astype(np.float32).astype(bf16)
        terms.append(term)
        rest = rest - term.astype(np.float64)
    return np.concatenate(terms, axis=0)


def gain_polynomial(degree):
    top = math.pi * math.pi

    def exact(t):
        t = np.asarray(t, np.float64)
        theta = np.sqrt(np.maximum(t, 1e-12))
        return np.where(t > 1e-10, (2.0 * np.sin(0.5 * theta) / theta) ** 2, 1.0)

    fit = np.polynomial.chebyshev.Chebyshev.interpolate(exact, degree, domain=[0.0, top * 1.0001])
    return [float(c) for c in fit.convert(kind=np.polynomial.Polynomial, domain=[-1, 1]).coef]


def row_mask():
    rows = lax.broadcasted_iota(jnp.int32, (GROUP, LANES), 0)
    lanes = lax.broadcasted_iota(jnp.int32, (GROUP, LANES), 1)
    return (lanes % GROUP == rows) & (lanes < USED)


def packed_lower_mask(shape):
    lanes = lax.broadcasted_iota(jnp.int32, shape, len(shape) - 1)
    tile = lanes // LANES
    inner = lanes % LANES
    plane = jnp.where(inner < USED, inner // GROUP, 2 * tile + (inner - USED) // GROUP)
    return plane < 3


def sections_kernel(now_ref, columns_ref, z_ref, *pack_refs):
    rows = now_ref.shape[0]
    count = len(pack_refs)
    group_x = rows // 4
    mask = row_mask()[None]
    lane = lax.broadcasted_iota(jnp.int32, (group_x, LANES), 1)
    halves = [[] for _ in pack_refs]
    for part in range(4):
        block = now_ref[part * group_x : (part + 1) * group_x]
        flat = block.reshape(group_x * block.shape[1], block.shape[2])
        section = jnp.dot(flat, columns_ref[...], preferred_element_type=jnp.float32)
        section = section.reshape(group_x, count, GROUP, LANES)
        for half in range(count):
            picked = jnp.sum(jnp.where(mask, section[:, half], 0.0), axis=1)
            picked = picked.astype(jnp.bfloat16)
            z_ref[part * group_x : (part + 1) * group_x, half * LANES : (half + 1) * LANES] = picked
            halves[half].append(picked.astype(jnp.float32))
    for half, pack_ref in enumerate(pack_refs):
        for tile in range(3):
            moved = pltpu.roll(halves[half][3], USED - 32 * tile, 1)
            pack_ref[:, tile * LANES : (tile + 1) * LANES] = jnp.where(
                lane < USED, halves[half][tile], moved
            ).astype(jnp.bfloat16)


def neighbours(face_ref, rect):
    partner = face_ref[rect]
    source = jnp.int32(0)
    for index in range(face_ref.shape[0]):
        source = source + jnp.where(face_ref[index] == rect, jnp.int32(index), jnp.int32(0))
    return partner, source


def forward_kernel(face_ref, place_ref, pack_a_ref, pack_b_ref, got_a_ref, got_b_ref, send_a_ref, send_b_ref):
    rect = place_ref[0]
    lower = packed_lower_mask(pack_a_ref.shape)
    for step, pack_ref, got_ref, send_ref in (
        (2, pack_a_ref, got_a_ref, send_a_ref),
        (1, pack_b_ref, got_b_ref, send_b_ref),
    ):
        partner, source = neighbours(face_ref, rect ^ step)
        own = pack_ref[...].astype(jnp.float32)
        got = got_ref[...].astype(jnp.float32)
        for_lower = jnp.where(partner == rect, own, got)
        for_upper = jnp.where(source == rect, own, got)
        send_ref[...] = jnp.where(lower, for_lower, for_upper).astype(jnp.bfloat16)


def pick(code, first, second, third):
    return jnp.where(code == 0, first, jnp.where(code == 1, second, third))


def forces_kernel(routed, face_ref, place_ref, z_ref, *refs):
    own_refs, one_refs, two_refs = [refs[i : len(refs) - 3 : 3] for i in range(3)]
    table_ref, near_ref, piece_ref = refs[-3:]
    count = len(own_refs)
    rect = place_ref[0]
    partner, source = neighbours(face_ref, rect)
    packed_rows = own_refs[0].shape[0]
    lower = packed_lower_mask(own_refs[0].shape)
    blocks = packed_rows // GROUP
    lane = lax.broadcasted_iota(jnp.int32, (blocks, GROUP, LANES), 2)
    for half, (own_ref, one_ref, two_ref) in enumerate(zip(own_refs, one_refs, two_refs)):
        if routed:
            step = half + 1
            code_lower = jnp.where(partner == rect, 0, jnp.where(partner == (rect ^ step), 1, 2))
            code_upper = jnp.where(source == rect, 0, jnp.where(source == (rect ^ step), 1, 2))
        else:
            code_lower, code_upper = jnp.int32(1), jnp.int32(2)
        values = [ref[...].astype(jnp.float32) for ref in (own_ref, one_ref, two_ref)]
        packed = jnp.where(lower, pick(code_lower, *values), pick(code_upper, *values))
        tiles = [
            packed[:, tile * LANES : (tile + 1) * LANES].reshape(blocks, GROUP, LANES) for tile in range(3)
        ]
        moved = [
            pltpu.roll(packed[:, tile * LANES : (tile + 1) * LANES], 32 * (tile + 1), 1).reshape(
                blocks, GROUP, LANES
            )
            for tile in range(3)
        ]
        last = jnp.where(lane < 32, moved[0], jnp.where(lane < 64, moved[1], moved[2]))
        for group, value in enumerate(tiles + [last]):
            value = jnp.where(lane < USED, value, 0.0).astype(jnp.bfloat16)
            for block in range(blocks):
                start = (block * 4 + group) * GROUP
                near_ref[start : start + GROUP, half * LANES : (half + 1) * LANES] = value[block]
    table = table_ref[...]

    def transform(ref, half):
        modes = ref[:, half * LANES : half * LANES + USED]
        out = lax.dot_general(modes, table, (((0,), (0,)), ((), ())), preferred_element_type=jnp.float32)
        out = out.astype(jnp.bfloat16).astype(jnp.float32)
        return [out[plane * GROUP : (plane + 1) * GROUP] for plane in range(PLANES)]

    for half in range(count):
        own = transform(z_ref, half)
        near = transform(near_ref, half)
        jump_up = [near[k] - own[5 - k] for k in range(3)]
        jump_down = [near[5 - k] - own[k] for k in range(3)]
        force = [None] * PLANES
        for m in range(3):
            down = coeffs[m] * jump_down[0]
            up = coeffs[m] * jump_up[0]
            for k in range(1, 3 - m):
                down = down + coeffs[m + k] * jump_down[k]
                up = up + coeffs[m + k] * jump_up[k]
            force[m] = courant_sq * down
            force[5 - m] = courant_sq * up
        width = piece_ref.shape[2] // PLANES
        for slot in range(piece_ref.shape[0]):
            parts = [plane[:, slot * width : (slot + 1) * width] for plane in force]
            piece_ref[slot, half * GROUP : (half + 1) * GROUP, :] = jnp.concatenate(parts, axis=1).astype(
                jnp.bfloat16
            )


def update_kernel(poly, sides, place_ref, now_ref, prev_ref, z_ref, near_ref, mix_ref, planes_ref, out_ref, force_ref):
    rows, local_y, depth_z = now_ref.shape
    step = pl.program_id(0)
    slab = place_ref[1]
    mask = row_mask()[None]
    for half in range(local_y // GROUP):
        cols = slice(half * LANES, (half + 1) * LANES)
        both = jnp.concatenate([z_ref[:, cols], near_ref[:, cols]], axis=1)
        modes = jnp.dot(
            jnp.concatenate([both, both, both], axis=1), mix_ref[...], preferred_element_type=jnp.float32
        )
        spread = jnp.where(mask, jnp.broadcast_to(modes[:, None, :], (rows, GROUP, LANES)), 0.0)
        spread = spread.astype(jnp.bfloat16).reshape(rows * GROUP, LANES)
        force = jnp.dot(spread, planes_ref[...], preferred_element_type=jnp.float32)
        force_ref[:, half * GROUP : (half + 1) * GROUP, :] = force.reshape(rows, GROUP, depth_z)
    scale = math.pi * math.pi / 3.0
    y_index = lax.broadcasted_iota(jnp.int32, (local_y, depth_z), 0) + slab * local_y
    z_index = lax.broadcasted_iota(jnp.int32, (local_y, depth_z), 1)
    y_part = y_index.astype(jnp.float32) / sides[1]
    z_part = z_index.astype(jnp.float32) / sides[2]
    base = scale * (y_part * y_part + z_part * z_part)

    def body(row, carry):
        x_index = jnp.full((1, 1), step * rows + row, jnp.int32)
        x_part = x_index.astype(jnp.float32) / sides[0]
        theta_sq = base + scale * (x_part * x_part)
        gain = poly[-1] * theta_sq + poly[-2]
        for coefficient in poly[-3::-1]:
            gain = gain * theta_sq + coefficient
        two_cos = 2.0 - theta_sq * gain
        value = two_cos * now_ref[row].astype(jnp.float32) - prev_ref[row].astype(jnp.float32)
        out_ref[row] = (value + gain * force_ref[row]).astype(jnp.bfloat16)
        return carry

    lax.fori_loop(0, rows, body, 0, unroll=2)


def planes_kernel(arrived_ref, table_ref, out_ref):
    out = lax.dot_general(
        arrived_ref[...], table_ref[...], (((0,), (0,)), ((), ())), preferred_element_type=jnp.float32
    )
    out_ref[...] = out


def smem():
    return pl.BlockSpec(memory_space=pltpu.SMEM)


def shards(modes_now, modes_prev, face_partner):
    slab_count = lax.axis_size("slab")
    rect_count = lax.axis_size("rect")
    slab_rank = lax.axis_index("slab")
    rect_rank = lax.axis_index("rect")
    _, length_x, local_y, depth_z = modes_now.shape
    length_y = local_y * slab_count
    local_x = length_x // slab_count
    assert local_y % GROUP == 0 and length_x % (4 * GROUP) == 0
    count = local_y // GROUP
    bf = jnp.bfloat16
    place = jnp.stack([rect_rank, slab_rank]).astype(jnp.int32)
    current = modes_now[0]
    earlier = modes_prev[0]
    columns = jnp.asarray(spread_columns(depth_z))
    planes = jnp.asarray(np.ascontiguousarray(spread_columns(depth_z).T))
    mix = jnp.asarray(force_matrix())
    table_x = jnp.asarray(cosine_table(length_x).astype(bf16))
    table_y = jnp.asarray(cosine_table(length_y).astype(bf16))

    block_x = 4 * GROUP
    packed = jax.ShapeDtypeStruct((length_x // 4, 3 * LANES), bf)
    z_own, *packs = pl.pallas_call(
        sections_kernel,
        grid=(length_x // block_x,),
        in_specs=[
            pl.BlockSpec((block_x, local_y, depth_z), lambda i: (i, 0, 0)),
            pl.BlockSpec((depth_z, LANES), lambda i: (0, 0)),
        ],
        out_specs=[
            pl.BlockSpec((block_x, count * LANES), lambda i: (i, 0)),
            *[pl.BlockSpec((GROUP, 3 * LANES), lambda i: (i, 0)) for _ in range(count)],
        ],
        out_shape=[jax.ShapeDtypeStruct((length_x, count * LANES), bf)] + [packed] * count,
        name="sections",
    )(current, columns)

    routed = rect_count == 4 and count == 2
    if routed:

        def hop(value, step):
            return lax.ppermute(value, "rect", [(j, j ^ step) for j in range(rect_count)])

        ones = [hop(packs[0], 1), hop(packs[1], 2)]
        sends = pl.pallas_call(
            forward_kernel,
            in_specs=[smem(), smem()] + [pl.BlockSpec() for _ in range(4)],
            out_shape=[packed, packed],
            name="forward",
        )(face_partner, place, *packs, *ones)
        twos = [hop(sends[0], 2), hop(sends[1], 1)]
    else:
        rect_ids = jnp.arange(rect_count, dtype=jnp.int32)
        partner = jnp.sum(jnp.where(rect_ids == rect_rank, face_partner, 0))
        source = jnp.sum(jnp.where(face_partner == rect_rank, rect_ids, 0))
        every = [lax.all_gather(pack, "rect", axis=0) for pack in packs]
        ones = [lax.dynamic_index_in_dim(value, partner, 0, keepdims=False) for value in every]
        twos = [lax.dynamic_index_in_dim(value, source, 0, keepdims=False) for value in every]
    routes = [value for triple in zip(packs, ones, twos) for value in triple]

    near, pieces = pl.pallas_call(
        functools.partial(forces_kernel, routed),
        in_specs=[smem(), smem()] + [pl.BlockSpec() for _ in range(2 + len(routes))],
        out_shape=[
            jax.ShapeDtypeStruct((length_x, count * LANES), bf),
            jax.ShapeDtypeStruct((slab_count, local_y, PLANES * local_x), bf),
        ],
        name="forces",
    )(face_partner, place, z_own, *routes, table_x)

    arrived = lax.all_to_all(pieces, "slab", split_axis=0, concat_axis=0, tiled=True)

    rows = 32
    fresh = pl.pallas_call(
        functools.partial(update_kernel, gain_polynomial(6), (length_x, length_y, depth_z)),
        grid=(length_x // rows,),
        in_specs=[
            smem(),
            pl.BlockSpec((rows, local_y, depth_z), lambda i: (i, 0, 0)),
            pl.BlockSpec((rows, local_y, depth_z), lambda i: (i, 0, 0)),
            pl.BlockSpec((rows, count * LANES), lambda i: (i, 0)),
            pl.BlockSpec((rows, count * LANES), lambda i: (i, 0)),
            pl.BlockSpec(mix.shape, lambda i: (0, 0)),
            pl.BlockSpec(planes.shape, lambda i: (0, 0)),
        ],
        out_specs=pl.BlockSpec((rows, local_y, depth_z), lambda i: (i, 0, 0)),
        out_shape=jax.ShapeDtypeStruct((length_x, local_y, depth_z), bf),
        scratch_shapes=[pltpu.VMEM((rows, local_y, depth_z), jnp.float32)],
        name="update",
    )(place, current, earlier, z_own, near, mix, planes)

    forcing = pl.pallas_call(
        planes_kernel,
        out_shape=jax.ShapeDtypeStruct((PLANES * local_x, length_y), jnp.float32),
        name="planes",
    )(arrived.reshape(length_y, PLANES * local_x), table_y)
    return (fresh[None], forcing.reshape(1, PLANES, local_x, length_y))


def solution(mesh):
    return jax.shard_map(
        shards,
        mesh=mesh,
        in_specs=(P("rect", None, "slab", None), P("rect", None, "slab", None), P()),
        out_specs=(P("rect", None, "slab", None), P("rect", None, "slab", None)),
        check_vma=False,
    )
```

```python
import functools
import math

import jax
import jax.numpy as jnp
import ml_dtypes
import numpy as np
from jax import lax
from jax.experimental import pallas as pl
from jax.experimental.pallas import tpu as pltpu
from jax.sharding import PartitionSpec as P

courant_sq = 1.0 / 3.0
coeffs = (1.5, -0.15, 2.0 / 180.0)
bf16 = ml_dtypes.bfloat16
PLANES = 6
LANES = 128
GROUP = 16
USED = PLANES * GROUP


def cosine_table(length):
    mode_index = np.arange(length, dtype=np.int64)[:, None]
    cell_index = np.arange(length, dtype=np.int64)[None, :]
    phase = mode_index * (2 * cell_index + 1) % (4 * length)
    angles = phase.astype(np.float32) * np.float32(math.pi / (2.0 * length))
    weights = np.where(mode_index == 0, math.sqrt(1.0 / length), math.sqrt(2.0 / length))
    return weights.astype(np.float32) * np.cos(angles)


def plane_columns(depth_z):
    table = cosine_table(depth_z)
    return np.concatenate([table[:, :3], table[:, depth_z - 3 :]], axis=1).astype(bf16)


def spread_columns(depth_z):
    columns = plane_columns(depth_z)
    out = np.zeros((depth_z, LANES), bf16)
    out[:, :USED] = np.repeat(columns, GROUP, axis=1)
    return out


def force_matrix():
    own = np.zeros((PLANES, PLANES), np.float64)
    other = np.zeros((PLANES, PLANES), np.float64)
    for m in range(3):
        for k in range(3 - m):
            weight = courant_sq * coeffs[m + k]
            other[5 - k, m] += weight
            own[k, m] -= weight
            other[k, 5 - m] += weight
            own[5 - k, 5 - m] -= weight
    full = np.zeros((2 * LANES, LANES), np.float64)
    for row in range(GROUP):
        full[row:USED:GROUP, row:USED:GROUP] = own
        full[LANES + row : LANES + USED : GROUP, row:USED:GROUP] = other
    terms = []
    rest = full
    for _ in range(3):
        term = rest.astype(np.float32).astype(bf16)
        terms.append(term)
        rest = rest - term.astype(np.float64)
    return np.concatenate(terms, axis=0)


def gain_polynomial(degree):
    top = math.pi * math.pi

    def exact(t):
        t = np.asarray(t, np.float64)
        theta = np.sqrt(np.maximum(t, 1e-12))
        return np.where(t > 1e-10, (2.0 * np.sin(0.5 * theta) / theta) ** 2, 1.0)

    fit = np.polynomial.chebyshev.Chebyshev.interpolate(exact, degree, domain=[0.0, top * 1.0001])
    return [float(c) for c in fit.convert(kind=np.polynomial.Polynomial, domain=[-1, 1]).coef]


def row_mask():
    rows = lax.broadcasted_iota(jnp.int32, (GROUP, LANES), 0)
    lanes = lax.broadcasted_iota(jnp.int32, (GROUP, LANES), 1)
    return (lanes % GROUP == rows) & (lanes < USED)


def packed_lower_mask(shape):
    lanes = lax.broadcasted_iota(jnp.int32, shape, len(shape) - 1)
    tile = lanes // LANES
    inner = lanes % LANES
    plane = jnp.where(inner < USED, inner // GROUP, 2 * tile + (inner - USED) // GROUP)
    return plane < 3


def gather_rows(section, row_of_lane, sublane):
    values = jnp.where((row_of_lane < 8)[None], section[:, :8], section[:, 8:])
    for distance in (4, 2, 1):
        count = values.shape[0] // 2
        first, second = values[:count], values[count:]
        early = ((sublane & distance) == 0)[None]
        late_row = ((row_of_lane & distance) != 0)[None]
        if distance == 4:
            kept = jnp.where(early, first, second)
            moved = pltpu.roll(jnp.where(early, second, first), 4, 1)
            values = jnp.where(early != late_row, kept, moved)
        else:
            up = pltpu.roll(first, 8 - distance, 1)
            down = pltpu.roll(second, distance, 1)
            values = jnp.where(early, jnp.where(late_row, up, first), jnp.where(late_row, second, down))
    return values[0]


def sections_kernel(now_ref, columns_ref, z_ref, *refs):
    *pack_refs, now_vmem, arrivals = refs
    count = len(pack_refs)
    chunks = arrivals.shape[0]
    length = now_ref.shape[0] // chunks

    def fetch(chunk):
        rows = pl.ds(chunk * length, length)
        return pltpu.make_async_copy(now_ref.at[rows], now_vmem.at[rows], arrivals.at[chunk])

    for chunk in range(chunks):
        fetch(chunk).start()
    sublane = lax.broadcasted_iota(jnp.int32, (8, LANES), 0)
    row_of_lane = lax.broadcasted_iota(jnp.int32, (8, LANES), 1) % GROUP
    lane = lax.broadcasted_iota(jnp.int32, (GROUP, LANES), 1)

    def body(step, carry):
        fetch(step).wait()
        halves = [[] for _ in pack_refs]
        for part in range(4):
            rows = pl.ds((step * 4 + part) * GROUP, GROUP)
            flat = now_vmem[rows].reshape(GROUP * now_vmem.shape[1], now_vmem.shape[2])
            section = jnp.dot(flat, columns_ref[...], preferred_element_type=jnp.float32)
            section = section.reshape(GROUP, count, GROUP, LANES)
            for half in range(count):
                picked = jnp.concatenate(
                    [gather_rows(section[i : i + 8, half], row_of_lane, sublane) for i in range(0, GROUP, 8)], axis=0
                ).astype(jnp.bfloat16)
                z_ref[rows, half * LANES : (half + 1) * LANES] = picked
                halves[half].append(picked.astype(jnp.float32))
        for half, pack_ref in enumerate(pack_refs):
            for tile in range(3):
                moved = pltpu.roll(halves[half][3], USED - 32 * tile, 1)
                pack_ref[pl.ds(step * GROUP, GROUP), tile * LANES : (tile + 1) * LANES] = jnp.where(
                    lane < USED, halves[half][tile], moved
                ).astype(jnp.bfloat16)
        return carry

    lax.fori_loop(0, chunks, body, 0)


def neighbours(face_ref, rect):
    partner = face_ref[rect]
    source = jnp.int32(0)
    for index in range(face_ref.shape[0]):
        source = source + jnp.where(face_ref[index] == rect, jnp.int32(index), jnp.int32(0))
    return partner, source


def forward_kernel(face_ref, pack_a_ref, pack_b_ref, got_a_ref, got_b_ref, send_a_ref, send_b_ref):
    rect = lax.axis_index("rect")
    lower = packed_lower_mask(pack_a_ref.shape)
    for step, pack_ref, got_ref, send_ref in (
        (2, pack_a_ref, got_a_ref, send_a_ref),
        (1, pack_b_ref, got_b_ref, send_b_ref),
    ):
        partner, source = neighbours(face_ref, rect ^ step)
        own = pack_ref[...].astype(jnp.float32)
        got = got_ref[...].astype(jnp.float32)
        for_lower = jnp.where(partner == rect, own, got)
        for_upper = jnp.where(source == rect, own, got)
        send_ref[...] = jnp.where(lower, for_lower, for_upper).astype(jnp.bfloat16)


def pick(code, first, second, third):
    return jnp.where(code == 0, first, jnp.where(code == 1, second, third))


def forces_kernel(routed, face_ref, z_ref, *refs):
    own_refs, one_refs, two_refs = [refs[i : len(refs) - 3 : 3] for i in range(3)]
    table_ref, near_ref, piece_ref = refs[-3:]
    count = len(own_refs)
    rect = lax.axis_index("rect")
    partner, source = neighbours(face_ref, rect)
    packed_rows = own_refs[0].shape[0]
    lower = packed_lower_mask(own_refs[0].shape)
    blocks = packed_rows // GROUP
    lane = lax.broadcasted_iota(jnp.int32, (blocks, GROUP, LANES), 2)
    for half, (own_ref, one_ref, two_ref) in enumerate(zip(own_refs, one_refs, two_refs)):
        if routed:
            step = half + 1
            code_lower = jnp.where(partner == rect, 0, jnp.where(partner == (rect ^ step), 1, 2))
            code_upper = jnp.where(source == rect, 0, jnp.where(source == (rect ^ step), 1, 2))
        else:
            code_lower, code_upper = jnp.int32(1), jnp.int32(2)
        values = [ref[...].astype(jnp.float32) for ref in (own_ref, one_ref, two_ref)]
        packed = jnp.where(lower, pick(code_lower, *values), pick(code_upper, *values))
        tiles = [
            packed[:, tile * LANES : (tile + 1) * LANES].reshape(blocks, GROUP, LANES) for tile in range(3)
        ]
        moved = [
            pltpu.roll(packed[:, tile * LANES : (tile + 1) * LANES], 32 * (tile + 1), 1).reshape(
                blocks, GROUP, LANES
            )
            for tile in range(3)
        ]
        last = jnp.where(lane < 32, moved[0], jnp.where(lane < 64, moved[1], moved[2]))
        for group, value in enumerate(tiles + [last]):
            value = jnp.where(lane < USED, value, 0.0).astype(jnp.bfloat16)
            for block in range(blocks):
                start = (block * 4 + group) * GROUP
                near_ref[start : start + GROUP, half * LANES : (half + 1) * LANES] = value[block]
    table = table_ref[...]

    def transform(ref, half):
        modes = ref[:, half * LANES : half * LANES + USED]
        out = lax.dot_general(modes, table, (((0,), (0,)), ((), ())), preferred_element_type=jnp.float32)
        out = out.astype(jnp.bfloat16).astype(jnp.float32)
        return [out[plane * GROUP : (plane + 1) * GROUP] for plane in range(PLANES)]

    for half in range(count):
        own = transform(z_ref, half)
        near = transform(near_ref, half)
        jump_up = [near[k] - own[5 - k] for k in range(3)]
        jump_down = [near[5 - k] - own[k] for k in range(3)]
        force = [None] * PLANES
        for m in range(3):
            down = coeffs[m] * jump_down[0]
            up = coeffs[m] * jump_up[0]
            for k in range(1, 3 - m):
                down = down + coeffs[m + k] * jump_down[k]
                up = up + coeffs[m + k] * jump_up[k]
            force[m] = courant_sq * down
            force[5 - m] = courant_sq * up
        width = piece_ref.shape[2] // PLANES
        for slot in range(piece_ref.shape[0]):
            parts = [plane[:, slot * width : (slot + 1) * width] for plane in force]
            piece_ref[slot, half * GROUP : (half + 1) * GROUP, :] = jnp.concatenate(parts, axis=1).astype(
                jnp.bfloat16
            )


def update_kernel(poly, sides, now_ref, prev_ref, z_ref, near_ref, mix_ref, planes_ref, out_ref, *scratch):
    now_vmem, prev_vmem, out_vmem, force_a, force_b, modes_ref, square_ref, arrivals, departures = scratch
    length_x, local_y, depth_z = now_vmem.shape
    chunks = departures.shape[0]
    length = length_x // chunks

    def rows_of(chunk):
        return pl.ds(chunk * length, length)

    def fetch(chunk):
        rows = rows_of(chunk)
        return [
            pltpu.make_async_copy(now_ref.at[rows], now_vmem.at[rows], arrivals.at[0, chunk]),
            pltpu.make_async_copy(prev_ref.at[rows], prev_vmem.at[rows], arrivals.at[1, chunk]),
        ]

    def send(chunk):
        rows = rows_of(chunk)
        return pltpu.make_async_copy(out_vmem.at[rows], out_ref.at[rows], departures.at[chunk])

    for chunk in range(chunks):
        for copy in fetch(chunk):
            copy.start()
    mask = row_mask()[None]
    for half in range(local_y // GROUP):
        cols = slice(half * LANES, (half + 1) * LANES)
        both = jnp.concatenate([z_ref[:, cols], near_ref[:, cols]], axis=1)
        modes_ref[:, cols] = jnp.dot(
            jnp.concatenate([both, both, both], axis=1), mix_ref[...], preferred_element_type=jnp.float32
        )
    scale = math.pi * math.pi / 3.0
    y_index = lax.broadcasted_iota(jnp.int32, (local_y, depth_z), 0) + lax.axis_index("slab") * local_y
    z_index = lax.broadcasted_iota(jnp.int32, (local_y, depth_z), 1)
    y_part = y_index.astype(jnp.float32) * (1.0 / sides[1])
    z_part = z_index.astype(jnp.float32) * (1.0 / sides[2])
    square_ref[...] = scale * (y_part * y_part + z_part * z_part)

    def x_square(x):
        part = x * (1.0 / sides[0])
        return scale * (part * part)

    def exact_gain(theta_sq):
        value = poly[-1] * theta_sq + poly[-2]
        for coefficient in poly[-3::-1]:
            value = value * theta_sq + coefficient
        return value

    groups = length_x // GROUP

    def make_force(group, force_ref):
        row = jnp.minimum(group, groups - 1) * GROUP
        for half in range(local_y // GROUP):
            modes = modes_ref[pl.ds(row, GROUP), half * LANES : (half + 1) * LANES]
            spread = jnp.where(mask, jnp.broadcast_to(modes[:, None, :], (GROUP, GROUP, LANES)), 0.0)
            spread = spread.astype(jnp.bfloat16).reshape(GROUP * GROUP, LANES)
            force = jnp.dot(spread, planes_ref[...], preferred_element_type=jnp.float32)
            force_ref[:, half * GROUP : (half + 1) * GROUP, :] = force.reshape(GROUP, GROUP, depth_z)

    middle = 0.5 * (GROUP - 1)
    reach = middle - 1.0
    begin, after = -middle / reach, (1.0 - middle) / reach

    def advance(group, force_ref):
        row = group * GROUP
        first = row.astype(jnp.float32)
        nodes = [x_square(first + (middle + offset)) for offset in (-reach, 0.0, reach)]
        x_sq = [x_square(first + float(step)) for step in range(GROUP)]
        for y_at in range(0, local_y, GROUP):
            for z_at in range(0, depth_z, LANES):
                tile = (slice(y_at, y_at + GROUP), slice(z_at, z_at + LANES))
                yz_sq = square_ref[tile]
                low, mid, high = [exact_gain(yz_sq + node) for node in nodes]
                slope = (high - low) * 0.5
                bend = (high + low) * 0.5 - mid
                gain = mid + begin * slope + (begin * begin) * bend
                rise = slope * (1.0 / reach) + bend * (after * after - begin * begin)
                turn = bend * (2.0 / (reach * reach))
                for step in range(GROUP):
                    at = (row + step,) + tile
                    two_cos = 2.0 - (yz_sq + x_sq[step]) * gain
                    value = two_cos * now_vmem[at].astype(jnp.float32) - prev_vmem[at].astype(jnp.float32)
                    out_vmem[at] = (value + gain * force_ref[(step,) + tile]).astype(jnp.bfloat16)
                    gain = gain + rise
                    rise = rise + turn

    make_force(0, force_a)
    pairs = length // (2 * GROUP)

    def whole(chunk, carry):
        for copy in fetch(chunk):
            copy.wait()

        def pair(index, inner):
            group = (chunk * pairs + index) * 2
            make_force(group + 1, force_b)
            advance(group, force_a)
            make_force(group + 2, force_a)
            advance(group + 1, force_b)
            return inner

        lax.fori_loop(0, pairs, pair, 0)
        send(chunk).start()
        return carry

    lax.fori_loop(0, chunks, whole, 0)
    for chunk in range(chunks):
        send(chunk).wait()


def planes_kernel(arrived_ref, table_ref, out_ref):
    out = lax.dot_general(
        arrived_ref[...], table_ref[...], (((0,), (0,)), ((), ())), preferred_element_type=jnp.float32
    )
    out_ref[...] = out


def smem():
    return pl.BlockSpec(memory_space=pltpu.SMEM)


def vmem():
    return pl.BlockSpec(memory_space=pltpu.VMEM)


def hbm():
    return pl.BlockSpec(memory_space=pltpu.HBM)


def limit(mib):
    return pltpu.CompilerParams(vmem_limit_bytes=mib << 20)


def shards(modes_now, modes_prev, face_partner):
    slab_count = lax.axis_size("slab")
    rect_count = lax.axis_size("rect")
    rect_rank = lax.axis_index("rect")
    _, length_x, local_y, depth_z = modes_now.shape
    length_y = local_y * slab_count
    local_x = length_x // slab_count
    assert local_y % GROUP == 0 and length_x % (4 * GROUP) == 0
    count = local_y // GROUP
    bf = jnp.bfloat16
    current = pltpu.with_memory_space_constraint(modes_now[0], pltpu.HBM)
    earlier = pltpu.with_memory_space_constraint(modes_prev[0], pltpu.HBM)
    columns = jnp.asarray(spread_columns(depth_z))
    planes = jnp.asarray(np.ascontiguousarray(spread_columns(depth_z).T))
    mix = jnp.asarray(force_matrix())
    table_x = jnp.asarray(cosine_table(length_x).astype(bf16))
    table_y = jnp.asarray(cosine_table(length_y).astype(bf16))

    packed = jax.ShapeDtypeStruct((length_x // 4, 3 * LANES), bf)
    chunks = 16
    z_own, *packs = pl.pallas_call(
        sections_kernel,
        in_specs=[hbm(), vmem()],
        out_specs=[vmem()] * (1 + count),
        out_shape=[jax.ShapeDtypeStruct((length_x, count * LANES), bf)] + [packed] * count,
        scratch_shapes=[
            pltpu.VMEM((length_x, local_y, depth_z), bf),
            pltpu.SemaphoreType.DMA((length_x // (4 * GROUP),)),
        ],
        compiler_params=limit(16),
        name="sections",
    )(current, columns)

    routed = rect_count == 4 and count == 2
    if routed:

        def hop(value, step):
            return lax.ppermute(value, "rect", [(j, j ^ step) for j in range(rect_count)])

        ones = [hop(packs[0], 1), hop(packs[1], 2)]
        sends = pl.pallas_call(
            forward_kernel,
            in_specs=[smem()] + [vmem()] * 4,
            out_specs=[vmem()] * 2,
            out_shape=[packed, packed],
            compiler_params=limit(8),
            name="forward",
        )(face_partner, *packs, *ones)
        twos = [hop(sends[0], 2), hop(sends[1], 1)]
    else:
        rect_ids = jnp.arange(rect_count, dtype=jnp.int32)
        partner = jnp.sum(jnp.where(rect_ids == rect_rank, face_partner, 0))
        source = jnp.sum(jnp.where(face_partner == rect_rank, rect_ids, 0))
        every = [lax.all_gather(pack, "rect", axis=0) for pack in packs]
        ones = [lax.dynamic_index_in_dim(value, partner, 0, keepdims=False) for value in every]
        twos = [lax.dynamic_index_in_dim(value, source, 0, keepdims=False) for value in every]
    routes = [value for triple in zip(packs, ones, twos) for value in triple]

    near, pieces = pl.pallas_call(
        functools.partial(forces_kernel, routed),
        in_specs=[smem()] + [vmem()] * (2 + len(routes)),
        out_specs=[vmem()] * 2,
        out_shape=[
            jax.ShapeDtypeStruct((length_x, count * LANES), bf),
            jax.ShapeDtypeStruct((slab_count, local_y, PLANES * local_x), bf),
        ],
        compiler_params=limit(8),
        name="forces",
    )(face_partner, z_own, *routes, table_x)

    arrived = lax.all_to_all(pieces, "slab", split_axis=0, concat_axis=0, tiled=True)

    wide = (length_x, local_y, depth_z)
    fresh = pl.pallas_call(
        functools.partial(update_kernel, gain_polynomial(5), (length_x, length_y, depth_z)),
        in_specs=[hbm(), hbm()] + [vmem()] * 4,
        out_specs=hbm(),
        out_shape=jax.ShapeDtypeStruct(wide, bf),
        scratch_shapes=[
            *[pltpu.VMEM(wide, bf)] * 3,
            *[pltpu.VMEM((GROUP, local_y, depth_z), jnp.float32)] * 2,
            pltpu.VMEM((length_x, count * LANES), jnp.float32),
            pltpu.VMEM((local_y, depth_z), jnp.float32),
            pltpu.SemaphoreType.DMA((2, chunks)),
            pltpu.SemaphoreType.DMA((chunks,)),
        ],
        compiler_params=limit(40),
        name="update",
    )(current, earlier, z_own, near, mix, planes)

    forcing = pl.pallas_call(
        planes_kernel,
        in_specs=[vmem()] * 2,
        out_specs=vmem(),
        out_shape=jax.ShapeDtypeStruct((PLANES * local_x, length_y), jnp.float32),
        compiler_params=limit(8),
        name="planes",
    )(arrived.reshape(length_y, PLANES * local_x), table_y)
    return (fresh[None], forcing.reshape(1, PLANES, local_x, length_y))


def solution(mesh):
    return jax.shard_map(
        shards,
        mesh=mesh,
        in_specs=(P("rect", None, "slab", None), P("rect", None, "slab", None), P()),
        out_specs=(P("rect", None, "slab", None), P("rect", None, "slab", None)),
        check_vma=False,
    )
```

```python
import functools
import math

import jax
import jax.numpy as jnp
import ml_dtypes
import numpy as np
from jax import lax
from jax.experimental import pallas as pl
from jax.experimental.pallas import tpu as pltpu
from jax.sharding import PartitionSpec as P

courant_sq = 1.0 / 3.0
coeffs = (1.5, -0.15, 2.0 / 180.0)
bf16 = ml_dtypes.bfloat16
PLANES = 6
LANES = 128
GROUP = 16
USED = PLANES * GROUP


def cosine_table(length):
    mode_index = np.arange(length, dtype=np.int64)[:, None]
    cell_index = np.arange(length, dtype=np.int64)[None, :]
    phase = mode_index * (2 * cell_index + 1) % (4 * length)
    angles = phase.astype(np.float32) * np.float32(math.pi / (2.0 * length))
    weights = np.where(mode_index == 0, math.sqrt(1.0 / length), math.sqrt(2.0 / length))
    return weights.astype(np.float32) * np.cos(angles)


def plane_columns(depth_z):
    table = cosine_table(depth_z)
    return np.concatenate([table[:, :3], table[:, depth_z - 3 :]], axis=1).astype(bf16)


def spread_columns(depth_z):
    columns = plane_columns(depth_z)
    out = np.zeros((depth_z, LANES), bf16)
    out[:, :USED] = np.repeat(columns, GROUP, axis=1)
    return out


def section_columns(depth_z):
    mode = lax.broadcasted_iota(jnp.int32, (depth_z, LANES), 0)
    lane = lax.broadcasted_iota(jnp.int32, (depth_z, LANES), 1)
    plane = lane // GROUP
    cell = jnp.where(plane < 3, plane, depth_z - PLANES + plane)
    phase = mode * (2 * cell + 1) % (4 * depth_z)
    angle = phase.astype(jnp.float32) * (math.pi / (2.0 * depth_z))
    weight = jnp.where(mode == 0, math.sqrt(1.0 / depth_z), math.sqrt(2.0 / depth_z))
    return jnp.where(lane < USED, weight * jnp.cos(angle), 0.0).astype(jnp.bfloat16)


def force_matrix():
    own = np.zeros((PLANES, PLANES), np.float64)
    other = np.zeros((PLANES, PLANES), np.float64)
    for m in range(3):
        for k in range(3 - m):
            weight = courant_sq * coeffs[m + k]
            other[5 - k, m] += weight
            own[k, m] -= weight
            other[k, 5 - m] += weight
            own[5 - k, 5 - m] -= weight
    full = np.zeros((2 * LANES, LANES), np.float64)
    for row in range(GROUP):
        full[row:USED:GROUP, row:USED:GROUP] = own
        full[LANES + row : LANES + USED : GROUP, row:USED:GROUP] = other
    terms = []
    rest = full
    for _ in range(3):
        term = rest.astype(np.float32).astype(bf16)
        terms.append(term)
        rest = rest - term.astype(np.float64)
    return np.concatenate(terms, axis=0)


def gain_polynomial(degree):
    top = math.pi * math.pi

    def exact(t):
        t = np.asarray(t, np.float64)
        theta = np.sqrt(np.maximum(t, 1e-12))
        return np.where(t > 1e-10, (2.0 * np.sin(0.5 * theta) / theta) ** 2, 1.0)

    fit = np.polynomial.chebyshev.Chebyshev.interpolate(exact, degree, domain=[0.0, top * 1.0001])
    return [float(c) for c in fit.convert(kind=np.polynomial.Polynomial, domain=[-1, 1]).coef]


def row_mask():
    rows = lax.broadcasted_iota(jnp.int32, (GROUP, LANES), 0)
    lanes = lax.broadcasted_iota(jnp.int32, (GROUP, LANES), 1)
    return (lanes % GROUP == rows) & (lanes < USED)


def packed_lower_mask(shape):
    lanes = lax.broadcasted_iota(jnp.int32, shape, len(shape) - 1)
    tile = lanes // LANES
    inner = lanes % LANES
    plane = jnp.where(inner < USED, inner // GROUP, 2 * tile + (inner - USED) // GROUP)
    return plane < 3


def gather_rows(section, row_of_lane, sublane):
    values = jnp.where((row_of_lane < 8)[None], section[:, :8], section[:, 8:])
    for distance in (4, 2, 1):
        count = values.shape[0] // 2
        first, second = values[:count], values[count:]
        early = ((sublane & distance) == 0)[None]
        late_row = ((row_of_lane & distance) != 0)[None]
        if distance == 4:
            kept = jnp.where(early, first, second)
            moved = pltpu.roll(jnp.where(early, second, first), 4, 1)
            values = jnp.where(early != late_row, kept, moved)
        else:
            up = pltpu.roll(first, 8 - distance, 1)
            down = pltpu.roll(second, distance, 1)
            values = jnp.where(early, jnp.where(late_row, up, first), jnp.where(late_row, second, down))
    return values[0]


def sections_kernel(now_ref, z_ref, pack_ref, now_vmem, arrivals):
    count = now_ref.shape[1] // GROUP
    packed_rows = now_ref.shape[0] // 4
    chunks = arrivals.shape[0]
    length = now_ref.shape[0] // chunks

    def fetch(chunk):
        rows = pl.ds(chunk * length, length)
        return pltpu.make_async_copy(now_ref.at[rows], now_vmem.at[rows], arrivals.at[chunk])

    for chunk in range(chunks):
        fetch(chunk).start()
    columns = section_columns(now_ref.shape[2])
    sublane = lax.broadcasted_iota(jnp.int32, (8, LANES), 0)
    row_of_lane = lax.broadcasted_iota(jnp.int32, (8, LANES), 1) % GROUP
    lane = lax.broadcasted_iota(jnp.int32, (GROUP, LANES), 1)

    def body(step, carry):
        fetch(step).wait()
        halves = [[] for _ in range(count)]
        for part in range(4):
            rows = pl.ds((step * 4 + part) * GROUP, GROUP)
            flat = now_vmem[rows].reshape(GROUP * now_vmem.shape[1], now_vmem.shape[2])
            section = jnp.dot(flat, columns, preferred_element_type=jnp.float32)
            section = section.reshape(GROUP, count, GROUP, LANES)
            for half in range(count):
                picked = jnp.concatenate(
                    [gather_rows(section[i : i + 8, half], row_of_lane, sublane) for i in range(0, GROUP, 8)], axis=0
                ).astype(jnp.bfloat16)
                z_ref[rows, half * LANES : (half + 1) * LANES] = picked
                halves[half].append(picked.astype(jnp.float32))
        for half in range(count):
            for tile in range(3):
                moved = pltpu.roll(halves[half][3], USED - 32 * tile, 1)
                pack_ref[pl.ds(half * packed_rows + step * GROUP, GROUP), tile * LANES : (tile + 1) * LANES] = jnp.where(
                    lane < USED, halves[half][tile], moved
                ).astype(jnp.bfloat16)
        return carry

    lax.fori_loop(0, chunks, body, 0)


def neighbours(face_ref, rect):
    partner = face_ref[rect]
    source = jnp.int32(0)
    for index in range(face_ref.shape[0]):
        source = source + jnp.where(face_ref[index] == rect, jnp.int32(index), jnp.int32(0))
    return partner, source


def forces_kernel(face_ref, z_ref, every_ref, table_ref, near_ref, piece_ref):
    count = z_ref.shape[1] // LANES
    partner, source = neighbours(face_ref, lax.axis_index("rect"))
    packed_rows = every_ref.shape[1] // count
    lower = packed_lower_mask((packed_rows, every_ref.shape[2]))
    blocks = packed_rows // GROUP
    lane = lax.broadcasted_iota(jnp.int32, (blocks, GROUP, LANES), 2)
    for half in range(count):
        rows = pl.ds(half * packed_rows, packed_rows)
        packed = jnp.where(
            lower, every_ref[partner, rows].astype(jnp.float32), every_ref[source, rows].astype(jnp.float32)
        )
        tiles = [
            packed[:, tile * LANES : (tile + 1) * LANES].reshape(blocks, GROUP, LANES) for tile in range(3)
        ]
        moved = [
            pltpu.roll(packed[:, tile * LANES : (tile + 1) * LANES], 32 * (tile + 1), 1).reshape(
                blocks, GROUP, LANES
            )
            for tile in range(3)
        ]
        last = jnp.where(lane < 32, moved[0], jnp.where(lane < 64, moved[1], moved[2]))
        for group, value in enumerate(tiles + [last]):
            value = jnp.where(lane < USED, value, 0.0).astype(jnp.bfloat16)
            for block in range(blocks):
                start = (block * 4 + group) * GROUP
                near_ref[start : start + GROUP, half * LANES : (half + 1) * LANES] = value[block]
    table = table_ref[...]

    def transform(ref, half):
        modes = ref[:, half * LANES : half * LANES + USED]
        out = lax.dot_general(modes, table, (((0,), (0,)), ((), ())), preferred_element_type=jnp.float32)
        out = out.astype(jnp.bfloat16).astype(jnp.float32)
        return [out[plane * GROUP : (plane + 1) * GROUP] for plane in range(PLANES)]

    for half in range(count):
        own = transform(z_ref, half)
        near = transform(near_ref, half)
        jump_up = [near[k] - own[5 - k] for k in range(3)]
        jump_down = [near[5 - k] - own[k] for k in range(3)]
        force = [None] * PLANES
        for m in range(3):
            down = coeffs[m] * jump_down[0]
            up = coeffs[m] * jump_up[0]
            for k in range(1, 3 - m):
                down = down + coeffs[m + k] * jump_down[k]
                up = up + coeffs[m + k] * jump_up[k]
            force[m] = courant_sq * down
            force[5 - m] = courant_sq * up
        width = piece_ref.shape[2] // PLANES
        for slot in range(piece_ref.shape[0]):
            parts = [plane[:, slot * width : (slot + 1) * width] for plane in force]
            piece_ref[slot, half * GROUP : (half + 1) * GROUP, :] = jnp.concatenate(parts, axis=1).astype(
                jnp.bfloat16
            )


def update_kernel(poly, sides, now_ref, prev_ref, z_ref, near_ref, mix_ref, planes_ref, out_ref, *scratch):
    now_vmem, prev_vmem, out_vmem, force_a, force_b, modes_ref, square_ref, arrivals, departures = scratch
    length_x, local_y, depth_z = now_vmem.shape
    chunks = departures.shape[0]
    length = length_x // chunks

    def rows_of(chunk):
        return pl.ds(chunk * length, length)

    def fetch(chunk):
        rows = rows_of(chunk)
        return [
            pltpu.make_async_copy(now_ref.at[rows], now_vmem.at[rows], arrivals.at[0, chunk]),
            pltpu.make_async_copy(prev_ref.at[rows], prev_vmem.at[rows], arrivals.at[1, chunk]),
        ]

    def send(chunk):
        rows = rows_of(chunk)
        return pltpu.make_async_copy(out_vmem.at[rows], out_ref.at[rows], departures.at[chunk])

    for chunk in range(chunks):
        for copy in fetch(chunk):
            copy.start()
    mask = row_mask()[None]
    for half in range(local_y // GROUP):
        cols = slice(half * LANES, (half + 1) * LANES)
        both = jnp.concatenate([z_ref[:, cols], near_ref[:, cols]], axis=1)
        modes_ref[:, cols] = jnp.dot(
            jnp.concatenate([both, both, both], axis=1), mix_ref[...], preferred_element_type=jnp.float32
        )
    scale = math.pi * math.pi / 3.0
    y_index = lax.broadcasted_iota(jnp.int32, (local_y, depth_z), 0) + lax.axis_index("slab") * local_y
    z_index = lax.broadcasted_iota(jnp.int32, (local_y, depth_z), 1)
    y_part = y_index.astype(jnp.float32) * (1.0 / sides[1])
    z_part = z_index.astype(jnp.float32) * (1.0 / sides[2])
    square_ref[...] = scale * (y_part * y_part + z_part * z_part)

    def x_square(x):
        part = x * (1.0 / sides[0])
        return scale * (part * part)

    def exact_gain(theta_sq):
        value = poly[-1] * theta_sq + poly[-2]
        for coefficient in poly[-3::-1]:
            value = value * theta_sq + coefficient
        return value

    groups = length_x // GROUP

    def make_force(group, force_ref):
        row = jnp.minimum(group, groups - 1) * GROUP
        for half in range(local_y // GROUP):
            modes = modes_ref[pl.ds(row, GROUP), half * LANES : (half + 1) * LANES]
            spread = jnp.where(mask, jnp.broadcast_to(modes[:, None, :], (GROUP, GROUP, LANES)), 0.0)
            spread = spread.astype(jnp.bfloat16).reshape(GROUP * GROUP, LANES)
            force = jnp.dot(spread, planes_ref[...], preferred_element_type=jnp.float32)
            force_ref[:, half * GROUP : (half + 1) * GROUP, :] = force.reshape(GROUP, GROUP, depth_z)

    middle = 0.5 * (GROUP - 1)
    reach = middle - 1.0
    begin, after = -middle / reach, (1.0 - middle) / reach

    def advance(group, force_ref):
        row = group * GROUP
        first = row.astype(jnp.float32)
        nodes = [x_square(first + (middle + offset)) for offset in (-reach, 0.0, reach)]
        x_sq = [x_square(first + float(step)) for step in range(GROUP)]
        for y_at in range(0, local_y, GROUP):
            for z_at in range(0, depth_z, LANES):
                tile = (slice(y_at, y_at + GROUP), slice(z_at, z_at + LANES))
                yz_sq = square_ref[tile]
                low, mid, high = [exact_gain(yz_sq + node) for node in nodes]
                slope = (high - low) * 0.5
                bend = (high + low) * 0.5 - mid
                gain = mid + begin * slope + (begin * begin) * bend
                rise = slope * (1.0 / reach) + bend * (after * after - begin * begin)
                turn = bend * (2.0 / (reach * reach))
                for step in range(GROUP):
                    at = (row + step,) + tile
                    two_cos = 2.0 - (yz_sq + x_sq[step]) * gain
                    value = two_cos * now_vmem[at].astype(jnp.float32) - prev_vmem[at].astype(jnp.float32)
                    out_vmem[at] = (value + gain * force_ref[(step,) + tile]).astype(jnp.bfloat16)
                    gain = gain + rise
                    rise = rise + turn

    make_force(0, force_a)
    pairs = length // (2 * GROUP)

    def whole(chunk, carry):
        for copy in fetch(chunk):
            copy.wait()

        def pair(index, inner):
            group = (chunk * pairs + index) * 2
            make_force(group + 1, force_b)
            advance(group, force_a)
            make_force(group + 2, force_a)
            advance(group + 1, force_b)
            return inner

        lax.fori_loop(0, pairs, pair, 0)
        send(chunk).start()
        return carry

    lax.fori_loop(0, chunks, whole, 0)
    for chunk in range(chunks):
        send(chunk).wait()


def planes_kernel(arrived_ref, table_ref, out_ref):
    out = lax.dot_general(
        arrived_ref[...], table_ref[...], (((0,), (0,)), ((), ())), preferred_element_type=jnp.float32
    )
    out_ref[...] = out


def smem():
    return pl.BlockSpec(memory_space=pltpu.SMEM)


def vmem():
    return pl.BlockSpec(memory_space=pltpu.VMEM)


def hbm():
    return pl.BlockSpec(memory_space=pltpu.HBM)


def limit(mib):
    return pltpu.CompilerParams(vmem_limit_bytes=mib << 20)


def shards(modes_now, modes_prev, face_partner):
    slab_count = lax.axis_size("slab")
    _, length_x, local_y, depth_z = modes_now.shape
    length_y = local_y * slab_count
    local_x = length_x // slab_count
    assert local_y % GROUP == 0 and length_x % (4 * GROUP) == 0
    count = local_y // GROUP
    bf = jnp.bfloat16
    current = pltpu.with_memory_space_constraint(modes_now[0], pltpu.HBM)
    earlier = pltpu.with_memory_space_constraint(modes_prev[0], pltpu.HBM)
    planes = jnp.asarray(np.ascontiguousarray(spread_columns(depth_z).T))
    mix = jnp.asarray(force_matrix())
    table_x = jnp.asarray(cosine_table(length_x).astype(bf16))
    table_y = jnp.asarray(cosine_table(length_y).astype(bf16))

    chunks = 16
    z_own, pack = pl.pallas_call(
        sections_kernel,
        in_specs=[hbm()],
        out_specs=[vmem()] * 2,
        out_shape=[
            jax.ShapeDtypeStruct((length_x, count * LANES), bf),
            jax.ShapeDtypeStruct((count * length_x // 4, 3 * LANES), bf),
        ],
        scratch_shapes=[
            pltpu.VMEM((length_x, local_y, depth_z), bf),
            pltpu.SemaphoreType.DMA((length_x // (4 * GROUP),)),
        ],
        compiler_params=limit(16),
        name="sections",
    )(current)

    every = lax.all_gather(pack, "rect", axis=0)
    near, pieces = pl.pallas_call(
        forces_kernel,
        in_specs=[smem()] + [vmem()] * 3,
        out_specs=[vmem()] * 2,
        out_shape=[
            jax.ShapeDtypeStruct((length_x, count * LANES), bf),
            jax.ShapeDtypeStruct((slab_count, local_y, PLANES * local_x), bf),
        ],
        compiler_params=limit(8),
        name="forces",
    )(face_partner, z_own, every, table_x)

    arrived = lax.all_to_all(pieces, "slab", split_axis=0, concat_axis=0, tiled=True)

    wide = (length_x, local_y, depth_z)
    fresh = pl.pallas_call(
        functools.partial(update_kernel, gain_polynomial(5), (length_x, length_y, depth_z)),
        in_specs=[hbm(), hbm()] + [vmem()] * 4,
        out_specs=hbm(),
        out_shape=jax.ShapeDtypeStruct(wide, bf),
        scratch_shapes=[
            *[pltpu.VMEM(wide, bf)] * 3,
            *[pltpu.VMEM((GROUP, local_y, depth_z), jnp.float32)] * 2,
            pltpu.VMEM((length_x, count * LANES), jnp.float32),
            pltpu.VMEM((local_y, depth_z), jnp.float32),
            pltpu.SemaphoreType.DMA((2, chunks)),
            pltpu.SemaphoreType.DMA((chunks,)),
        ],
        compiler_params=limit(40),
        name="update",
    )(current, earlier, z_own, near, mix, planes)

    forcing = pl.pallas_call(
        planes_kernel,
        in_specs=[vmem()] * 2,
        out_specs=vmem(),
        out_shape=jax.ShapeDtypeStruct((PLANES * local_x, length_y), jnp.float32),
        compiler_params=limit(8),
        name="planes",
    )(arrived.reshape(length_y, PLANES * local_x), table_y)
    return (fresh[None], forcing.reshape(1, PLANES, local_x, length_y))


def solution(mesh):
    return jax.shard_map(
        shards,
        mesh=mesh,
        in_specs=(P("rect", None, "slab", None), P("rect", None, "slab", None), P()),
        out_specs=(P("rect", None, "slab", None), P("rect", None, "slab", None)),
        check_vma=False,
    )
```

```python
import functools
import math

import jax
import jax.numpy as jnp
import ml_dtypes
import numpy as np
from jax import lax
from jax.experimental import pallas as pl
from jax.experimental.pallas import tpu as pltpu
from jax.sharding import PartitionSpec as P

courant_sq = 1.0 / 3.0
coeffs = (1.5, -0.15, 2.0 / 180.0)
bf16 = ml_dtypes.bfloat16
PLANES = 6
LANES = 128
GROUP = 16
USED = PLANES * GROUP
UNROLL = 2
SECTION_CHUNKS = 4
DIRECT = ()


def cosine_table(length):
    mode_index = np.arange(length, dtype=np.int64)[:, None]
    cell_index = np.arange(length, dtype=np.int64)[None, :]
    phase = mode_index * (2 * cell_index + 1) % (4 * length)
    angles = phase.astype(np.float32) * np.float32(math.pi / (2.0 * length))
    weights = np.where(mode_index == 0, math.sqrt(1.0 / length), math.sqrt(2.0 / length))
    return weights.astype(np.float32) * np.cos(angles)


def plane_columns(depth_z):
    table = cosine_table(depth_z)
    return np.concatenate([table[:, :3], table[:, depth_z - 3 :]], axis=1).astype(bf16)


def spread_columns(depth_z):
    columns = plane_columns(depth_z)
    out = np.zeros((depth_z, LANES), bf16)
    out[:, :USED] = np.repeat(columns, GROUP, axis=1)
    return out


def section_columns(depth_z):
    mode = lax.broadcasted_iota(jnp.int32, (depth_z, LANES), 0)
    lane = lax.broadcasted_iota(jnp.int32, (depth_z, LANES), 1)
    plane = lane // GROUP
    cell = jnp.where(plane < 3, plane, depth_z - PLANES + plane)
    phase = mode * (2 * cell + 1) % (4 * depth_z)
    angle = phase.astype(jnp.float32) * (math.pi / (2.0 * depth_z))
    weight = jnp.where(mode == 0, math.sqrt(1.0 / depth_z), math.sqrt(2.0 / depth_z))
    return jnp.where(lane < USED, weight * jnp.cos(angle), 0.0).astype(jnp.bfloat16)


def force_matrix():
    own = np.zeros((PLANES, PLANES), np.float64)
    other = np.zeros((PLANES, PLANES), np.float64)
    for m in range(3):
        for k in range(3 - m):
            weight = courant_sq * coeffs[m + k]
            other[5 - k, m] += weight
            own[k, m] -= weight
            other[k, 5 - m] += weight
            own[5 - k, 5 - m] -= weight
    full = np.zeros((2 * LANES, LANES), np.float64)
    for row in range(GROUP):
        full[row:USED:GROUP, row:USED:GROUP] = own
        full[LANES + row : LANES + USED : GROUP, row:USED:GROUP] = other
    terms = []
    rest = full
    for _ in range(3):
        term = rest.astype(np.float32).astype(bf16)
        terms.append(term)
        rest = rest - term.astype(np.float64)
    return np.concatenate(terms, axis=0)


def gain_polynomial(degree):
    top = math.pi * math.pi

    def exact(t):
        t = np.asarray(t, np.float64)
        theta = np.sqrt(np.maximum(t, 1e-12))
        return np.where(t > 1e-10, (2.0 * np.sin(0.5 * theta) / theta) ** 2, 1.0)

    fit = np.polynomial.chebyshev.Chebyshev.interpolate(exact, degree, domain=[0.0, top * 1.0001])
    return [float(c) for c in fit.convert(kind=np.polynomial.Polynomial, domain=[-1, 1]).coef]


def row_mask():
    rows = lax.broadcasted_iota(jnp.int32, (GROUP, LANES), 0)
    lanes = lax.broadcasted_iota(jnp.int32, (GROUP, LANES), 1)
    return (lanes % GROUP == rows) & (lanes < USED)


def packed_lower_mask(shape):
    lanes = lax.broadcasted_iota(jnp.int32, shape, len(shape) - 1)
    tile = lanes // LANES
    inner = lanes % LANES
    plane = jnp.where(inner < USED, inner // GROUP, 2 * tile + (inner - USED) // GROUP)
    return plane < 3


def gather_rows(section, row_of_lane, sublane):
    values = jnp.where((row_of_lane < 8)[None], section[:, :8], section[:, 8:])
    for distance in (4, 2, 1):
        count = values.shape[0] // 2
        first, second = values[:count], values[count:]
        early = ((sublane & distance) == 0)[None]
        late_row = ((row_of_lane & distance) != 0)[None]
        if distance == 4:
            kept = jnp.where(early, first, second)
            moved = pltpu.roll(jnp.where(early, second, first), 4, 1)
            values = jnp.where(early != late_row, kept, moved)
        else:
            up = pltpu.roll(first, 8 - distance, 1)
            down = pltpu.roll(second, distance, 1)
            values = jnp.where(early, jnp.where(late_row, up, first), jnp.where(late_row, second, down))
    return values[0]


def sections_kernel(now_ref, z_ref, pack_ref, now_vmem, arrivals):
    count = now_ref.shape[1] // GROUP
    packed_rows = now_ref.shape[0] // 4
    chunks = arrivals.shape[0]
    length = now_ref.shape[0] // chunks

    def fetch(chunk):
        rows = pl.ds(chunk * length, length)
        return pltpu.make_async_copy(now_ref.at[rows], now_vmem.at[rows], arrivals.at[chunk])

    for chunk in range(chunks):
        fetch(chunk).start()
    columns = section_columns(now_ref.shape[2])
    sublane = lax.broadcasted_iota(jnp.int32, (8, LANES), 0)
    row_of_lane = lax.broadcasted_iota(jnp.int32, (8, LANES), 1) % GROUP
    lane = lax.broadcasted_iota(jnp.int32, (GROUP, LANES), 1)

    def step_rows(step):
        halves = [[] for _ in range(count)]
        for part in range(4):
            rows = pl.ds((step * 4 + part) * GROUP, GROUP)
            flat = now_vmem[rows].reshape(GROUP * now_vmem.shape[1], now_vmem.shape[2])
            section = jnp.dot(flat, columns, preferred_element_type=jnp.float32)
            section = section.reshape(GROUP, count, GROUP, LANES)
            for half in range(count):
                picked = jnp.concatenate(
                    [gather_rows(section[i : i + 8, half], row_of_lane, sublane) for i in range(0, GROUP, 8)], axis=0
                ).astype(jnp.bfloat16)
                z_ref[rows, half * LANES : (half + 1) * LANES] = picked
                halves[half].append(picked.astype(jnp.float32))
        for half in range(count):
            for tile in range(3):
                moved = pltpu.roll(halves[half][3], USED - 32 * tile, 1)
                pack_ref[pl.ds(half * packed_rows + step * GROUP, GROUP), tile * LANES : (tile + 1) * LANES] = jnp.where(
                    lane < USED, halves[half][tile], moved
                ).astype(jnp.bfloat16)

    steps = length // (4 * GROUP)

    def body(chunk, carry):
        fetch(chunk).wait()
        for step in range(steps):
            step_rows(chunk * steps + step)
        return carry

    lax.fori_loop(0, chunks, body, 0)


def neighbours(face_ref, rect):
    partner = face_ref[rect]
    source = jnp.int32(0)
    for index in range(face_ref.shape[0]):
        source = source + jnp.where(face_ref[index] == rect, jnp.int32(index), jnp.int32(0))
    return partner, source


def forces_kernel(face_ref, z_ref, *refs):
    *every_refs, table_ref, near_ref, piece_ref = refs
    count = z_ref.shape[1] // LANES
    rect = lax.axis_index("rect")
    partner, source = neighbours(face_ref, rect)
    packed_rows = every_refs[0].shape[-2] // count
    lower = packed_lower_mask((packed_rows, every_refs[0].shape[-1]))

    def pack_of(other, rows):
        if len(every_refs) == 1:
            return every_refs[0][other, rows].astype(jnp.float32)
        value = every_refs[0][rows].astype(jnp.float32)
        for distance, ref in enumerate(every_refs[1:], 1):
            value = jnp.where(other == (rect ^ distance), ref[rows].astype(jnp.float32), value)
        return value

    blocks = packed_rows // GROUP
    lane = lax.broadcasted_iota(jnp.int32, (blocks, GROUP, LANES), 2)
    for half in range(count):
        rows = pl.ds(half * packed_rows, packed_rows)
        packed = jnp.where(lower, pack_of(partner, rows), pack_of(source, rows))
        tiles = [
            packed[:, tile * LANES : (tile + 1) * LANES].reshape(blocks, GROUP, LANES) for tile in range(3)
        ]
        moved = [
            pltpu.roll(packed[:, tile * LANES : (tile + 1) * LANES], 32 * (tile + 1), 1).reshape(
                blocks, GROUP, LANES
            )
            for tile in range(3)
        ]
        last = jnp.where(lane < 32, moved[0], jnp.where(lane < 64, moved[1], moved[2]))
        for group, value in enumerate(tiles + [last]):
            value = jnp.where(lane < USED, value, 0.0).astype(jnp.bfloat16)
            for block in range(blocks):
                start = (block * 4 + group) * GROUP
                near_ref[start : start + GROUP, half * LANES : (half + 1) * LANES] = value[block]
    modes = jnp.concatenate([z_ref[...], near_ref[...]], axis=1)
    cells = lax.dot_general(
        modes, table_ref[...], (((0,), (0,)), ((), ())), preferred_element_type=jnp.float32
    )
    cells = cells.astype(jnp.bfloat16).astype(jnp.float32)

    def sections_of(tile):
        return [cells[tile * LANES + p * GROUP : tile * LANES + (p + 1) * GROUP] for p in range(PLANES)]

    for half in range(count):
        own = sections_of(half)
        near = sections_of(count + half)
        jump_up = [near[k] - own[5 - k] for k in range(3)]
        jump_down = [near[5 - k] - own[k] for k in range(3)]
        force = [None] * PLANES
        for m in range(3):
            down = coeffs[m] * jump_down[0]
            up = coeffs[m] * jump_up[0]
            for k in range(1, 3 - m):
                down = down + coeffs[m + k] * jump_down[k]
                up = up + coeffs[m + k] * jump_up[k]
            force[m] = courant_sq * down
            force[5 - m] = courant_sq * up
        width = piece_ref.shape[2] // PLANES
        for slot in range(piece_ref.shape[0]):
            parts = [plane[:, slot * width : (slot + 1) * width] for plane in force]
            piece_ref[slot, half * GROUP : (half + 1) * GROUP, :] = jnp.concatenate(parts, axis=1).astype(
                jnp.bfloat16
            )


def update_kernel(poly, sides, now_ref, prev_ref, z_ref, near_ref, mix_ref, planes_ref, out_ref, *scratch):
    now_vmem, prev_vmem, out_vmem, force_a, force_b, modes_ref, square_ref, arrivals, departures = scratch
    length_x, local_y, depth_z = now_vmem.shape
    chunks = departures.shape[0]
    length = length_x // chunks

    def rows_of(chunk):
        return pl.ds(chunk * length, length)

    def fetch(chunk):
        rows = rows_of(chunk)
        return [
            pltpu.make_async_copy(now_ref.at[rows], now_vmem.at[rows], arrivals.at[0, chunk]),
            pltpu.make_async_copy(prev_ref.at[rows], prev_vmem.at[rows], arrivals.at[1, chunk]),
        ]

    def send(chunk):
        rows = rows_of(chunk)
        return pltpu.make_async_copy(out_vmem.at[rows], out_ref.at[rows], departures.at[chunk])

    for chunk in range(chunks):
        for copy in fetch(chunk):
            copy.start()
    mask = row_mask()[None]
    for half in range(local_y // GROUP):
        cols = slice(half * LANES, (half + 1) * LANES)
        both = jnp.concatenate([z_ref[:, cols], near_ref[:, cols]], axis=1)
        modes_ref[:, cols] = jnp.dot(
            jnp.concatenate([both, both, both], axis=1), mix_ref[...], preferred_element_type=jnp.float32
        )
    scale = math.pi * math.pi / 3.0
    y_index = lax.broadcasted_iota(jnp.int32, (local_y, depth_z), 0) + lax.axis_index("slab") * local_y
    z_index = lax.broadcasted_iota(jnp.int32, (local_y, depth_z), 1)
    y_part = y_index.astype(jnp.float32) * (1.0 / sides[1])
    z_part = z_index.astype(jnp.float32) * (1.0 / sides[2])
    square_ref[...] = scale * (y_part * y_part + z_part * z_part)

    def x_square(x):
        part = x * (1.0 / sides[0])
        return scale * (part * part)

    def exact_gain(theta_sq):
        value = poly[-1] * theta_sq + poly[-2]
        for coefficient in poly[-3::-1]:
            value = value * theta_sq + coefficient
        return value

    groups = length_x // GROUP

    def make_force(group, force_ref):
        row = jnp.minimum(group, groups - 1) * GROUP
        for half in range(local_y // GROUP):
            modes = modes_ref[pl.ds(row, GROUP), half * LANES : (half + 1) * LANES]
            spread = jnp.where(mask, jnp.broadcast_to(modes[:, None, :], (GROUP, GROUP, LANES)), 0.0)
            spread = spread.astype(jnp.bfloat16).reshape(GROUP * GROUP, LANES)
            force = jnp.dot(spread, planes_ref[...], preferred_element_type=jnp.float32)
            force_ref[:, half * GROUP : (half + 1) * GROUP, :] = force.reshape(GROUP, GROUP, depth_z)

    middle = 0.5 * (GROUP - 1)
    reach = middle - 1.0
    begin, after = -middle / reach, (1.0 - middle) / reach

    def advance(group, force_ref):
        row = group * GROUP
        first = row.astype(jnp.float32)
        nodes = [x_square(first + (middle + offset)) for offset in (-reach, 0.0, reach)]
        x_sq = [x_square(first + float(step)) for step in range(GROUP)]
        for y_at in range(0, local_y, GROUP):
            for z_at in range(0, depth_z, LANES):
                tile = (slice(y_at, y_at + GROUP), slice(z_at, z_at + LANES))
                yz_sq = square_ref[tile]
                low, mid, high = [exact_gain(yz_sq + node) for node in nodes]
                slope = (high - low) * 0.5
                bend = (high + low) * 0.5 - mid
                gain = mid + begin * slope + (begin * begin) * bend
                rise = slope * (1.0 / reach) + bend * (after * after - begin * begin)
                turn = bend * (2.0 / (reach * reach))
                for step in range(GROUP):
                    at = (row + step,) + tile
                    two_cos = 2.0 - (yz_sq + x_sq[step]) * gain
                    value = two_cos * now_vmem[at].astype(jnp.float32) - prev_vmem[at].astype(jnp.float32)
                    out_vmem[at] = (value + gain * force_ref[(step,) + tile]).astype(jnp.bfloat16)
                    gain = gain + rise
                    rise = rise + turn

    make_force(0, force_a)
    pairs = length // (2 * GROUP)

    def whole(chunk, carry):
        for copy in fetch(chunk):
            copy.wait()

        def pair(index, inner):
            group = (chunk * pairs + index) * 2
            make_force(group + 1, force_b)
            advance(group, force_a)
            make_force(group + 2, force_a)
            advance(group + 1, force_b)
            return inner

        lax.fori_loop(0, pairs, pair, 0, unroll=UNROLL)
        send(chunk).start()
        return carry

    lax.fori_loop(0, chunks, whole, 0)
    for chunk in range(chunks):
        send(chunk).wait()


def planes_kernel(arrived_ref, table_ref, out_ref):
    out = lax.dot_general(
        arrived_ref[...], table_ref[...], (((0,), (0,)), ((), ())), preferred_element_type=jnp.float32
    )
    out_ref[...] = out


def smem():
    return pl.BlockSpec(memory_space=pltpu.SMEM)


def vmem():
    return pl.BlockSpec(memory_space=pltpu.VMEM)


def hbm():
    return pl.BlockSpec(memory_space=pltpu.HBM)


def limit(mib):
    return pltpu.CompilerParams(vmem_limit_bytes=mib << 20)


def shards(modes_now, modes_prev, face_partner):
    slab_count = lax.axis_size("slab")
    _, length_x, local_y, depth_z = modes_now.shape
    length_y = local_y * slab_count
    local_x = length_x // slab_count
    assert local_y % GROUP == 0 and length_x % (4 * GROUP) == 0
    count = local_y // GROUP
    bf = jnp.bfloat16
    current = pltpu.with_memory_space_constraint(modes_now[0], pltpu.HBM)
    earlier = pltpu.with_memory_space_constraint(modes_prev[0], pltpu.HBM)
    planes = jnp.asarray(np.ascontiguousarray(spread_columns(depth_z).T))
    mix = jnp.asarray(force_matrix())
    table_x = jnp.asarray(cosine_table(length_x).astype(bf16))
    table_y = jnp.asarray(cosine_table(length_y).astype(bf16))

    chunks = 8
    z_own, pack = pl.pallas_call(
        sections_kernel,
        in_specs=[hbm()],
        out_specs=[vmem()] * 2,
        out_shape=[
            jax.ShapeDtypeStruct((length_x, count * LANES), bf),
            jax.ShapeDtypeStruct((count * length_x // 4, 3 * LANES), bf),
        ],
        scratch_shapes=[
            pltpu.VMEM((length_x, local_y, depth_z), bf),
            pltpu.SemaphoreType.DMA((SECTION_CHUNKS,)),
        ],
        compiler_params=limit(16),
        name="sections",
    )(current)

    rect_count = lax.axis_size("rect")
    if rect_count in DIRECT:
        every = [pack]
        for distance in range(1, rect_count):
            pairs = [(j, j ^ distance) for j in range(rect_count)]
            every.append(lax.ppermute(pack, "rect", pairs))
    else:
        every = [lax.all_gather(pack, "rect", axis=0)]
    near, pieces = pl.pallas_call(
        forces_kernel,
        in_specs=[smem()] + [vmem()] * (2 + len(every)),
        out_specs=[vmem()] * 2,
        out_shape=[
            jax.ShapeDtypeStruct((length_x, count * LANES), bf),
            jax.ShapeDtypeStruct((slab_count, local_y, PLANES * local_x), bf),
        ],
        compiler_params=limit(8),
        name="forces",
    )(face_partner, z_own, *every, table_x)

    arrived = lax.all_to_all(pieces, "slab", split_axis=0, concat_axis=0, tiled=True)

    wide = (length_x, local_y, depth_z)
    fresh = pl.pallas_call(
        functools.partial(update_kernel, gain_polynomial(5), (length_x, length_y, depth_z)),
        in_specs=[hbm(), hbm()] + [vmem()] * 4,
        out_specs=hbm(),
        out_shape=jax.ShapeDtypeStruct(wide, bf),
        scratch_shapes=[
            *[pltpu.VMEM(wide, bf)] * 3,
            *[pltpu.VMEM((GROUP, local_y, depth_z), jnp.float32)] * 2,
            pltpu.VMEM((length_x, count * LANES), jnp.float32),
            pltpu.VMEM((local_y, depth_z), jnp.float32),
            pltpu.SemaphoreType.DMA((2, chunks)),
            pltpu.SemaphoreType.DMA((chunks,)),
        ],
        compiler_params=limit(40),
        name="update",
    )(current, earlier, z_own, near, mix, planes)

    forcing = pl.pallas_call(
        planes_kernel,
        in_specs=[vmem()] * 2,
        out_specs=vmem(),
        out_shape=jax.ShapeDtypeStruct((PLANES * local_x, length_y), jnp.float32),
        compiler_params=limit(8),
        name="planes",
    )(arrived.reshape(length_y, PLANES * local_x), table_y)
    return (fresh[None], forcing.reshape(1, PLANES, local_x, length_y))


def solution(mesh):
    return jax.shard_map(
        shards,
        mesh=mesh,
        in_specs=(P("rect", None, "slab", None), P("rect", None, "slab", None), P()),
        out_specs=(P("rect", None, "slab", None), P("rect", None, "slab", None)),
        check_vma=False,
    )
```

```python
import functools
import math

import jax
import jax.numpy as jnp
import ml_dtypes
import numpy as np
from jax import lax
from jax.experimental import pallas as pl
from jax.experimental.pallas import tpu as pltpu
from jax.sharding import PartitionSpec as P

courant_sq = 1.0 / 3.0
coeffs = (1.5, -0.15, 2.0 / 180.0)
bf16 = ml_dtypes.bfloat16
PLANES = 6
LANES = 128
GROUP = 16
USED = PLANES * GROUP
SECTION_CHUNKS = 4
DIRECT = ()


def cosine_table(length):
    mode_index = np.arange(length, dtype=np.int64)[:, None]
    cell_index = np.arange(length, dtype=np.int64)[None, :]
    phase = mode_index * (2 * cell_index + 1) % (4 * length)
    angles = phase.astype(np.float32) * np.float32(math.pi / (2.0 * length))
    weights = np.where(mode_index == 0, math.sqrt(1.0 / length), math.sqrt(2.0 / length))
    return weights.astype(np.float32) * np.cos(angles)


def plane_columns(depth_z):
    table = cosine_table(depth_z)
    return np.concatenate([table[:, :3], table[:, depth_z - 3 :]], axis=1).astype(bf16)


def spread_columns(depth_z):
    columns = plane_columns(depth_z)
    out = np.zeros((depth_z, LANES), bf16)
    out[:, :USED] = np.repeat(columns, GROUP, axis=1)
    return out


def section_columns(depth_z):
    mode = lax.broadcasted_iota(jnp.int32, (depth_z, LANES), 0)
    lane = lax.broadcasted_iota(jnp.int32, (depth_z, LANES), 1)
    plane = lane // GROUP
    cell = jnp.where(plane < 3, plane, depth_z - PLANES + plane)
    phase = mode * (2 * cell + 1) % (4 * depth_z)
    angle = phase.astype(jnp.float32) * (math.pi / (2.0 * depth_z))
    weight = jnp.where(mode == 0, math.sqrt(1.0 / depth_z), math.sqrt(2.0 / depth_z))
    return jnp.where(lane < USED, weight * jnp.cos(angle), 0.0).astype(jnp.bfloat16)


def force_matrix():
    own = np.zeros((PLANES, PLANES), np.float64)
    other = np.zeros((PLANES, PLANES), np.float64)
    for m in range(3):
        for k in range(3 - m):
            weight = courant_sq * coeffs[m + k]
            other[5 - k, m] += weight
            own[k, m] -= weight
            other[k, 5 - m] += weight
            own[5 - k, 5 - m] -= weight
    full = np.zeros((2 * LANES, LANES), np.float64)
    for row in range(GROUP):
        full[row:USED:GROUP, row:USED:GROUP] = own
        full[LANES + row : LANES + USED : GROUP, row:USED:GROUP] = other
    terms = []
    rest = full
    for _ in range(3):
        term = rest.astype(np.float32).astype(bf16)
        terms.append(term)
        rest = rest - term.astype(np.float64)
    return np.concatenate(terms, axis=0)


def gain_polynomial(degree):
    top = math.pi * math.pi

    def exact(t):
        t = np.asarray(t, np.float64)
        theta = np.sqrt(np.maximum(t, 1e-12))
        return np.where(t > 1e-10, (2.0 * np.sin(0.5 * theta) / theta) ** 2, 1.0)

    fit = np.polynomial.chebyshev.Chebyshev.interpolate(exact, degree, domain=[0.0, top * 1.0001])
    return [float(c) for c in fit.convert(kind=np.polynomial.Polynomial, domain=[-1, 1]).coef]


def row_mask():
    rows = lax.broadcasted_iota(jnp.int32, (GROUP, LANES), 0)
    lanes = lax.broadcasted_iota(jnp.int32, (GROUP, LANES), 1)
    return (lanes % GROUP == rows) & (lanes < USED)


def packed_lower_mask(shape):
    lanes = lax.broadcasted_iota(jnp.int32, shape, len(shape) - 1)
    tile = lanes // LANES
    inner = lanes % LANES
    plane = jnp.where(inner < USED, inner // GROUP, 2 * tile + (inner - USED) // GROUP)
    return plane < 3


def gather_rows(section, row_of_lane, sublane):
    values = jnp.where((row_of_lane < 8)[None], section[:, :8], section[:, 8:])
    for distance in (4, 2, 1):
        count = values.shape[0] // 2
        first, second = values[:count], values[count:]
        early = ((sublane & distance) == 0)[None]
        late_row = ((row_of_lane & distance) != 0)[None]
        if distance == 4:
            kept = jnp.where(early, first, second)
            moved = pltpu.roll(jnp.where(early, second, first), 4, 1)
            values = jnp.where(early != late_row, kept, moved)
        else:
            up = pltpu.roll(first, 8 - distance, 1)
            down = pltpu.roll(second, distance, 1)
            values = jnp.where(early, jnp.where(late_row, up, first), jnp.where(late_row, second, down))
    return values[0]


def sections_kernel(now_ref, prev_ref, z_ref, pack_ref, first_now_ref, first_prev_ref, now_vmem, arrivals, extras):
    count = now_ref.shape[1] // GROUP
    packed_rows = now_ref.shape[0] // 4
    chunks = arrivals.shape[0]
    length = now_ref.shape[0] // chunks

    def fetch(chunk):
        rows = pl.ds(chunk * length, length)
        return pltpu.make_async_copy(now_ref.at[rows], now_vmem.at[rows], arrivals.at[chunk])

    for chunk in range(chunks):
        fetch(chunk).start()
    first = pl.ds(0, first_now_ref.shape[0])
    keeps = [
        pltpu.make_async_copy(now_ref.at[first], first_now_ref, extras.at[0]),
        pltpu.make_async_copy(prev_ref.at[first], first_prev_ref, extras.at[1]),
    ]
    for copy in keeps:
        copy.start()
    columns = section_columns(now_ref.shape[2])
    sublane = lax.broadcasted_iota(jnp.int32, (8, LANES), 0)
    row_of_lane = lax.broadcasted_iota(jnp.int32, (8, LANES), 1) % GROUP
    lane = lax.broadcasted_iota(jnp.int32, (GROUP, LANES), 1)

    def step_rows(step):
        halves = [[] for _ in range(count)]
        for part in range(4):
            rows = pl.ds((step * 4 + part) * GROUP, GROUP)
            flat = now_vmem[rows].reshape(GROUP * now_vmem.shape[1], now_vmem.shape[2])
            section = jnp.dot(flat, columns, preferred_element_type=jnp.float32)
            section = section.reshape(GROUP, count, GROUP, LANES)
            for half in range(count):
                picked = jnp.concatenate(
                    [gather_rows(section[i : i + 8, half], row_of_lane, sublane) for i in range(0, GROUP, 8)], axis=0
                ).astype(jnp.bfloat16)
                z_ref[rows, half * LANES : (half + 1) * LANES] = picked
                halves[half].append(picked.astype(jnp.float32))
        for half in range(count):
            for tile in range(3):
                moved = pltpu.roll(halves[half][3], USED - 32 * tile, 1)
                pack_ref[pl.ds(half * packed_rows + step * GROUP, GROUP), tile * LANES : (tile + 1) * LANES] = jnp.where(
                    lane < USED, halves[half][tile], moved
                ).astype(jnp.bfloat16)

    steps = length // (4 * GROUP)

    def body(chunk, carry):
        fetch(chunk).wait()
        for step in range(steps):
            step_rows(chunk * steps + step)
        return carry

    lax.fori_loop(0, chunks, body, 0)
    for copy in keeps:
        copy.wait()


def neighbours(face_ref, rect):
    partner = face_ref[rect]
    source = jnp.int32(0)
    for index in range(face_ref.shape[0]):
        source = source + jnp.where(face_ref[index] == rect, jnp.int32(index), jnp.int32(0))
    return partner, source


def forces_kernel(face_ref, z_ref, *refs):
    *every_refs, table_ref, near_ref, piece_ref = refs
    count = z_ref.shape[1] // LANES
    rect = lax.axis_index("rect")
    partner, source = neighbours(face_ref, rect)
    packed_rows = every_refs[0].shape[-2] // count
    lower = packed_lower_mask((packed_rows, every_refs[0].shape[-1]))

    def pack_of(other, rows):
        if len(every_refs) == 1:
            return every_refs[0][other, rows].astype(jnp.float32)
        value = every_refs[0][rows].astype(jnp.float32)
        for distance, ref in enumerate(every_refs[1:], 1):
            value = jnp.where(other == (rect ^ distance), ref[rows].astype(jnp.float32), value)
        return value

    blocks = packed_rows // GROUP
    lane = lax.broadcasted_iota(jnp.int32, (blocks, GROUP, LANES), 2)
    for half in range(count):
        rows = pl.ds(half * packed_rows, packed_rows)
        packed = jnp.where(lower, pack_of(partner, rows), pack_of(source, rows))
        tiles = [
            packed[:, tile * LANES : (tile + 1) * LANES].reshape(blocks, GROUP, LANES) for tile in range(3)
        ]
        moved = [
            pltpu.roll(packed[:, tile * LANES : (tile + 1) * LANES], 32 * (tile + 1), 1).reshape(
                blocks, GROUP, LANES
            )
            for tile in range(3)
        ]
        last = jnp.where(lane < 32, moved[0], jnp.where(lane < 64, moved[1], moved[2]))
        for group, value in enumerate(tiles + [last]):
            value = jnp.where(lane < USED, value, 0.0).astype(jnp.bfloat16)
            for block in range(blocks):
                start = (block * 4 + group) * GROUP
                near_ref[start : start + GROUP, half * LANES : (half + 1) * LANES] = value[block]
    modes = jnp.concatenate([z_ref[...], near_ref[...]], axis=1)
    cells = lax.dot_general(
        modes, table_ref[...], (((0,), (0,)), ((), ())), preferred_element_type=jnp.float32
    )
    cells = cells.astype(jnp.bfloat16).astype(jnp.float32)

    def sections_of(tile):
        return [cells[tile * LANES + p * GROUP : tile * LANES + (p + 1) * GROUP] for p in range(PLANES)]

    for half in range(count):
        own = sections_of(half)
        near = sections_of(count + half)
        jump_up = [near[k] - own[5 - k] for k in range(3)]
        jump_down = [near[5 - k] - own[k] for k in range(3)]
        force = [None] * PLANES
        for m in range(3):
            down = coeffs[m] * jump_down[0]
            up = coeffs[m] * jump_up[0]
            for k in range(1, 3 - m):
                down = down + coeffs[m + k] * jump_down[k]
                up = up + coeffs[m + k] * jump_up[k]
            force[m] = courant_sq * down
            force[5 - m] = courant_sq * up
        width = piece_ref.shape[2] // PLANES
        for slot in range(piece_ref.shape[0]):
            parts = [plane[:, slot * width : (slot + 1) * width] for plane in force]
            piece_ref[slot, half * GROUP : (half + 1) * GROUP, :] = jnp.concatenate(parts, axis=1).astype(
                jnp.bfloat16
            )


def update_kernel(poly, sides, now_ref, prev_ref, first_now_ref, first_prev_ref, z_ref, near_ref, mix_ref, planes_ref, out_ref, *scratch):
    now_vmem, prev_vmem, out_vmem, force_a, force_b, modes_ref, square_ref, arrivals, departures = scratch
    length_x, local_y, depth_z = now_vmem.shape
    chunks = arrivals.shape[1]
    length = length_x // chunks

    def rows_of(chunk):
        return pl.ds(chunk * length, length)

    def fetch(chunk):
        rows = rows_of(chunk)
        return [
            pltpu.make_async_copy(now_ref.at[rows], now_vmem.at[rows], arrivals.at[0, chunk]),
            pltpu.make_async_copy(prev_ref.at[rows], prev_vmem.at[rows], arrivals.at[1, chunk]),
        ]

    pieces = departures.shape[0] // chunks

    def send(piece):
        rows = pl.ds(piece * (length // pieces), length // pieces)
        return pltpu.make_async_copy(out_vmem.at[rows], out_ref.at[rows], departures.at[piece])

    for chunk in range(1, chunks):
        for copy in fetch(chunk):
            copy.start()
    mask = row_mask()[None]
    for half in range(local_y // GROUP):
        cols = slice(half * LANES, (half + 1) * LANES)
        both = jnp.concatenate([z_ref[:, cols], near_ref[:, cols]], axis=1)
        modes_ref[:, cols] = jnp.dot(
            jnp.concatenate([both, both, both], axis=1), mix_ref[...], preferred_element_type=jnp.float32
        )
    scale = math.pi * math.pi / 3.0
    y_index = lax.broadcasted_iota(jnp.int32, (local_y, depth_z), 0) + lax.axis_index("slab") * local_y
    z_index = lax.broadcasted_iota(jnp.int32, (local_y, depth_z), 1)
    y_part = y_index.astype(jnp.float32) * (1.0 / sides[1])
    z_part = z_index.astype(jnp.float32) * (1.0 / sides[2])
    square_ref[...] = scale * (y_part * y_part + z_part * z_part)

    def x_square(x):
        part = x * (1.0 / sides[0])
        return scale * (part * part)

    def exact_gain(theta_sq):
        value = poly[-1] * theta_sq + poly[-2]
        for coefficient in poly[-3::-1]:
            value = value * theta_sq + coefficient
        return value

    groups = length_x // GROUP

    def make_force(group, force_ref):
        row = jnp.minimum(group, groups - 1) * GROUP
        for half in range(local_y // GROUP):
            modes = modes_ref[pl.ds(row, GROUP), half * LANES : (half + 1) * LANES]
            spread = jnp.where(mask, jnp.broadcast_to(modes[:, None, :], (GROUP, GROUP, LANES)), 0.0)
            spread = spread.astype(jnp.bfloat16).reshape(GROUP * GROUP, LANES)
            force = jnp.dot(spread, planes_ref[...], preferred_element_type=jnp.float32)
            force_ref[:, half * GROUP : (half + 1) * GROUP, :] = force.reshape(GROUP, GROUP, depth_z)

    middle = 0.5 * (GROUP - 1)
    reach = middle - 1.0
    begin, after = -middle / reach, (1.0 - middle) / reach

    def advance(group, force_ref, now_vmem, prev_vmem):
        row = group * GROUP
        first = row.astype(jnp.float32)
        nodes = [x_square(first + (middle + offset)) for offset in (-reach, 0.0, reach)]
        x_sq = [x_square(first + float(step)) for step in range(GROUP)]
        for y_at in range(0, local_y, GROUP):
            for z_at in range(0, depth_z, LANES):
                tile = (slice(y_at, y_at + GROUP), slice(z_at, z_at + LANES))
                yz_sq = square_ref[tile]
                low, mid, high = [exact_gain(yz_sq + node) for node in nodes]
                slope = (high - low) * 0.5
                bend = (high + low) * 0.5 - mid
                gain = mid + begin * slope + (begin * begin) * bend
                rise = slope * (1.0 / reach) + bend * (after * after - begin * begin)
                turn = bend * (2.0 / (reach * reach))
                for step in range(GROUP):
                    at = (row + step,) + tile
                    two_cos = 2.0 - (yz_sq + x_sq[step]) * gain
                    value = two_cos * now_vmem[at].astype(jnp.float32) - prev_vmem[at].astype(jnp.float32)
                    out_vmem[at] = (value + gain * force_ref[(step,) + tile]).astype(jnp.bfloat16)
                    gain = gain + rise
                    rise = rise + turn

    make_force(0, force_a)
    pairs = length // (2 * GROUP)

    def compute(chunk, now_rows, prev_rows):
        for index in range(pairs):
            group = (chunk * pairs + index) * 2
            make_force(group + 1, force_b)
            advance(group, force_a, now_rows, prev_rows)
            make_force(group + 2, force_a)
            advance(group + 1, force_b, now_rows, prev_rows)
            if (index + 1) * pieces % pairs == 0:
                send(chunk * pieces + (index + 1) * pieces // pairs - 1).start()

    def whole(chunk, carry):
        for copy in fetch(chunk):
            copy.wait()
        compute(chunk, now_vmem, prev_vmem)
        return carry

    compute(jnp.int32(0), first_now_ref, first_prev_ref)
    lax.fori_loop(1, chunks, whole, 0)
    for piece in range(pieces * chunks):
        send(piece).wait()


def planes_kernel(arrived_ref, table_ref, out_ref):
    out = lax.dot_general(
        arrived_ref[...], table_ref[...], (((0,), (0,)), ((), ())), preferred_element_type=jnp.float32
    )
    out_ref[...] = out


def smem():
    return pl.BlockSpec(memory_space=pltpu.SMEM)


def vmem():
    return pl.BlockSpec(memory_space=pltpu.VMEM)


def hbm():
    return pl.BlockSpec(memory_space=pltpu.HBM)


def limit(mib):
    return pltpu.CompilerParams(vmem_limit_bytes=mib << 20)


def shards(modes_now, modes_prev, face_partner):
    slab_count = lax.axis_size("slab")
    _, length_x, local_y, depth_z = modes_now.shape
    length_y = local_y * slab_count
    local_x = length_x // slab_count
    assert local_y % GROUP == 0 and length_x % (4 * GROUP) == 0
    count = local_y // GROUP
    bf = jnp.bfloat16
    current = pltpu.with_memory_space_constraint(modes_now[0], pltpu.HBM)
    earlier = pltpu.with_memory_space_constraint(modes_prev[0], pltpu.HBM)
    planes = jnp.asarray(np.ascontiguousarray(spread_columns(depth_z).T))
    mix = jnp.asarray(force_matrix())
    table_x = jnp.asarray(cosine_table(length_x).astype(bf16))
    table_y = jnp.asarray(cosine_table(length_y).astype(bf16))

    chunks = 8
    first_rows = jax.ShapeDtypeStruct((length_x // chunks, local_y, depth_z), bf)
    z_own, pack, first_now, first_prev = pl.pallas_call(
        sections_kernel,
        in_specs=[hbm()] * 2,
        out_specs=[vmem()] * 4,
        out_shape=[
            jax.ShapeDtypeStruct((length_x, count * LANES), bf),
            jax.ShapeDtypeStruct((count * length_x // 4, 3 * LANES), bf),
            first_rows,
            first_rows,
        ],
        scratch_shapes=[
            pltpu.VMEM((length_x, local_y, depth_z), bf),
            pltpu.SemaphoreType.DMA((SECTION_CHUNKS,)),
            pltpu.SemaphoreType.DMA((2,)),
        ],
        compiler_params=limit(16),
        name="sections",
    )(current, earlier)

    rect_count = lax.axis_size("rect")
    if rect_count in DIRECT:
        every = [pack]
        for distance in range(1, rect_count):
            pairs = [(j, j ^ distance) for j in range(rect_count)]
            every.append(lax.ppermute(pack, "rect", pairs))
    else:
        every = [lax.all_gather(pack, "rect", axis=0)]
    near, pieces = pl.pallas_call(
        forces_kernel,
        in_specs=[smem()] + [vmem()] * (2 + len(every)),
        out_specs=[vmem()] * 2,
        out_shape=[
            jax.ShapeDtypeStruct((length_x, count * LANES), bf),
            jax.ShapeDtypeStruct((slab_count, local_y, PLANES * local_x), bf),
        ],
        compiler_params=limit(8),
        name="forces",
    )(face_partner, z_own, *every, table_x)

    arrived = lax.all_to_all(pieces, "slab", split_axis=0, concat_axis=0, tiled=True)

    wide = (length_x, local_y, depth_z)
    fresh = pl.pallas_call(
        functools.partial(update_kernel, gain_polynomial(5), (length_x, length_y, depth_z)),
        in_specs=[hbm(), hbm()] + [vmem()] * 6,
        out_specs=hbm(),
        out_shape=jax.ShapeDtypeStruct(wide, bf),
        scratch_shapes=[
            *[pltpu.VMEM(wide, bf)] * 3,
            *[pltpu.VMEM((GROUP, local_y, depth_z), jnp.float32)] * 2,
            pltpu.VMEM((length_x, count * LANES), jnp.float32),
            pltpu.VMEM((local_y, depth_z), jnp.float32),
            pltpu.SemaphoreType.DMA((2, chunks)),
            pltpu.SemaphoreType.DMA((2 * chunks,)),
        ],
        compiler_params=limit(40),
        name="update",
    )(current, earlier, first_now, first_prev, z_own, near, mix, planes)

    forcing = pl.pallas_call(
        planes_kernel,
        in_specs=[vmem()] * 2,
        out_specs=vmem(),
        out_shape=jax.ShapeDtypeStruct((PLANES * local_x, length_y), jnp.float32),
        compiler_params=limit(8),
        name="planes",
    )(arrived.reshape(length_y, PLANES * local_x), table_y)
    return (fresh[None], forcing.reshape(1, PLANES, local_x, length_y))


def solution(mesh):
    return jax.shard_map(
        shards,
        mesh=mesh,
        in_specs=(P("rect", None, "slab", None), P("rect", None, "slab", None), P()),
        out_specs=(P("rect", None, "slab", None), P("rect", None, "slab", None)),
        check_vma=False,
    )
```

```python
import functools
import math

import jax
import jax.numpy as jnp
import ml_dtypes
import numpy as np
from jax import lax
from jax.experimental import pallas as pl
from jax.experimental.pallas import tpu as pltpu
from jax.sharding import PartitionSpec as P

courant_sq = 1.0 / 3.0
coeffs = (1.5, -0.15, 2.0 / 180.0)
bf16 = ml_dtypes.bfloat16
PLANES = 6
LANES = 128
GROUP = 16
USED = PLANES * GROUP
SECTION_CHUNKS = 4
DIRECT = ()


def cosine_table(length):
    mode_index = np.arange(length, dtype=np.int64)[:, None]
    cell_index = np.arange(length, dtype=np.int64)[None, :]
    phase = mode_index * (2 * cell_index + 1) % (4 * length)
    angles = phase.astype(np.float32) * np.float32(math.pi / (2.0 * length))
    weights = np.where(mode_index == 0, math.sqrt(1.0 / length), math.sqrt(2.0 / length))
    return weights.astype(np.float32) * np.cos(angles)


def plane_columns(depth_z):
    table = cosine_table(depth_z)
    return np.concatenate([table[:, :3], table[:, depth_z - 3 :]], axis=1).astype(bf16)


def spread_columns(depth_z):
    columns = plane_columns(depth_z)
    out = np.zeros((depth_z, LANES), bf16)
    out[:, :USED] = np.repeat(columns, GROUP, axis=1)
    return out


def section_columns(depth_z):
    mode = lax.broadcasted_iota(jnp.int32, (depth_z, LANES), 0)
    lane = lax.broadcasted_iota(jnp.int32, (depth_z, LANES), 1)
    plane = lane // GROUP
    cell = jnp.where(plane < 3, plane, depth_z - PLANES + plane)
    phase = mode * (2 * cell + 1) % (4 * depth_z)
    angle = phase.astype(jnp.float32) * (math.pi / (2.0 * depth_z))
    weight = jnp.where(mode == 0, math.sqrt(1.0 / depth_z), math.sqrt(2.0 / depth_z))
    return jnp.where(lane < USED, weight * jnp.cos(angle), 0.0).astype(jnp.bfloat16)


def force_matrix():
    own = np.zeros((PLANES, PLANES), np.float64)
    other = np.zeros((PLANES, PLANES), np.float64)
    for m in range(3):
        for k in range(3 - m):
            weight = courant_sq * coeffs[m + k]
            other[5 - k, m] += weight
            own[k, m] -= weight
            other[k, 5 - m] += weight
            own[5 - k, 5 - m] -= weight
    full = np.zeros((2 * LANES, LANES), np.float64)
    for row in range(GROUP):
        full[row:USED:GROUP, row:USED:GROUP] = own
        full[LANES + row : LANES + USED : GROUP, row:USED:GROUP] = other
    terms = []
    rest = full
    for _ in range(3):
        term = rest.astype(np.float32).astype(bf16)
        terms.append(term)
        rest = rest - term.astype(np.float64)
    return np.concatenate(terms, axis=0)


def gain_polynomial(degree):
    top = math.pi * math.pi

    def exact(t):
        t = np.asarray(t, np.float64)
        theta = np.sqrt(np.maximum(t, 1e-12))
        return np.where(t > 1e-10, (2.0 * np.sin(0.5 * theta) / theta) ** 2, 1.0)

    fit = np.polynomial.chebyshev.Chebyshev.interpolate(exact, degree, domain=[0.0, top * 1.0001])
    return [float(c) for c in fit.convert(kind=np.polynomial.Polynomial, domain=[-1, 1]).coef]


def row_mask():
    rows = lax.broadcasted_iota(jnp.int32, (GROUP, LANES), 0)
    lanes = lax.broadcasted_iota(jnp.int32, (GROUP, LANES), 1)
    return (lanes % GROUP == rows) & (lanes < USED)


def packed_lower_mask(shape):
    lanes = lax.broadcasted_iota(jnp.int32, shape, len(shape) - 1)
    tile = lanes // LANES
    inner = lanes % LANES
    plane = jnp.where(inner < USED, inner // GROUP, 2 * tile + (inner - USED) // GROUP)
    return plane < 3


def gather_rows(section, row_of_lane, sublane):
    values = jnp.where((row_of_lane < 8)[None], section[:, :8], section[:, 8:])
    for distance in (4, 2, 1):
        count = values.shape[0] // 2
        first, second = values[:count], values[count:]
        early = ((sublane & distance) == 0)[None]
        late_row = ((row_of_lane & distance) != 0)[None]
        if distance == 4:
            kept = jnp.where(early, first, second)
            moved = pltpu.roll(jnp.where(early, second, first), 4, 1)
            values = jnp.where(early != late_row, kept, moved)
        else:
            up = pltpu.roll(first, 8 - distance, 1)
            down = pltpu.roll(second, distance, 1)
            values = jnp.where(early, jnp.where(late_row, up, first), jnp.where(late_row, second, down))
    return values[0]


def sections_kernel(now_ref, prev_ref, z_ref, pack_ref, first_now_ref, first_prev_ref, now_vmem, arrivals, extras):
    count = now_ref.shape[1] // GROUP
    packed_rows = now_ref.shape[0] // 4
    chunks = arrivals.shape[0]
    length = now_ref.shape[0] // chunks

    def fetch(chunk):
        rows = pl.ds(chunk * length, length)
        return pltpu.make_async_copy(now_ref.at[rows], now_vmem.at[rows], arrivals.at[chunk])

    for chunk in range(chunks):
        fetch(chunk).start()
    first = pl.ds(0, first_now_ref.shape[0])
    keeps = [
        pltpu.make_async_copy(now_ref.at[first], first_now_ref, extras.at[0]),
        pltpu.make_async_copy(prev_ref.at[first], first_prev_ref, extras.at[1]),
    ]
    for copy in keeps:
        copy.start()
    columns = section_columns(now_ref.shape[2])
    sublane = lax.broadcasted_iota(jnp.int32, (8, LANES), 0)
    row_of_lane = lax.broadcasted_iota(jnp.int32, (8, LANES), 1) % GROUP
    lane = lax.broadcasted_iota(jnp.int32, (GROUP, LANES), 1)

    def step_rows(step):
        halves = [[] for _ in range(count)]
        for part in range(4):
            rows = pl.ds((step * 4 + part) * GROUP, GROUP)
            flat = now_vmem[rows].reshape(GROUP * now_vmem.shape[1], now_vmem.shape[2])
            section = jnp.dot(flat, columns, preferred_element_type=jnp.float32)
            section = section.reshape(GROUP, count, GROUP, LANES)
            for half in range(count):
                picked = jnp.concatenate(
                    [gather_rows(section[i : i + 8, half], row_of_lane, sublane) for i in range(0, GROUP, 8)], axis=0
                ).astype(jnp.bfloat16)
                z_ref[rows, half * LANES : (half + 1) * LANES] = picked
                halves[half].append(picked.astype(jnp.float32))
        for half in range(count):
            for tile in range(3):
                moved = pltpu.roll(halves[half][3], USED - 32 * tile, 1)
                pack_ref[pl.ds(half * packed_rows + step * GROUP, GROUP), tile * LANES : (tile + 1) * LANES] = jnp.where(
                    lane < USED, halves[half][tile], moved
                ).astype(jnp.bfloat16)

    steps = length // (4 * GROUP)

    def body(chunk, carry):
        fetch(chunk).wait()
        for step in range(steps):
            step_rows(chunk * steps + step)
        return carry

    lax.fori_loop(0, chunks, body, 0)
    for copy in keeps:
        copy.wait()


def neighbours(face_ref, rect):
    partner = face_ref[rect]
    source = jnp.int32(0)
    for index in range(face_ref.shape[0]):
        source = source + jnp.where(face_ref[index] == rect, jnp.int32(index), jnp.int32(0))
    return partner, source


def forces_kernel(face_ref, z_ref, *refs):
    *every_refs, table_ref, near_ref, piece_ref = refs
    count = z_ref.shape[1] // LANES
    rect = lax.axis_index("rect")
    partner, source = neighbours(face_ref, rect)
    packed_rows = every_refs[0].shape[-2] // count
    lower = packed_lower_mask((packed_rows, every_refs[0].shape[-1]))

    def pack_of(other, rows):
        if len(every_refs) == 1:
            return every_refs[0][other, rows].astype(jnp.float32)
        value = every_refs[0][rows].astype(jnp.float32)
        for distance, ref in enumerate(every_refs[1:], 1):
            value = jnp.where(other == (rect ^ distance), ref[rows].astype(jnp.float32), value)
        return value

    blocks = packed_rows // GROUP
    lane = lax.broadcasted_iota(jnp.int32, (blocks, GROUP, LANES), 2)
    for half in range(count):
        rows = pl.ds(half * packed_rows, packed_rows)
        packed = jnp.where(lower, pack_of(partner, rows), pack_of(source, rows))
        tiles = [
            packed[:, tile * LANES : (tile + 1) * LANES].reshape(blocks, GROUP, LANES) for tile in range(3)
        ]
        moved = [
            pltpu.roll(packed[:, tile * LANES : (tile + 1) * LANES], 32 * (tile + 1), 1).reshape(
                blocks, GROUP, LANES
            )
            for tile in range(3)
        ]
        last = jnp.where(lane < 32, moved[0], jnp.where(lane < 64, moved[1], moved[2]))
        for group, value in enumerate(tiles + [last]):
            value = jnp.where(lane < USED, value, 0.0).astype(jnp.bfloat16)
            for block in range(blocks):
                start = (block * 4 + group) * GROUP
                near_ref[start : start + GROUP, half * LANES : (half + 1) * LANES] = value[block]
    modes = jnp.concatenate([z_ref[...], near_ref[...]], axis=1)
    cells = lax.dot_general(
        modes, table_ref[...], (((0,), (0,)), ((), ())), preferred_element_type=jnp.float32
    )
    cells = cells.astype(jnp.bfloat16).astype(jnp.float32)

    def sections_of(tile):
        return [cells[tile * LANES + p * GROUP : tile * LANES + (p + 1) * GROUP] for p in range(PLANES)]

    for half in range(count):
        own = sections_of(half)
        near = sections_of(count + half)
        jump_up = [near[k] - own[5 - k] for k in range(3)]
        jump_down = [near[5 - k] - own[k] for k in range(3)]
        force = [None] * PLANES
        for m in range(3):
            down = coeffs[m] * jump_down[0]
            up = coeffs[m] * jump_up[0]
            for k in range(1, 3 - m):
                down = down + coeffs[m + k] * jump_down[k]
                up = up + coeffs[m + k] * jump_up[k]
            force[m] = courant_sq * down
            force[5 - m] = courant_sq * up
        width = piece_ref.shape[2] // PLANES
        for slot in range(piece_ref.shape[0]):
            parts = [plane[:, slot * width : (slot + 1) * width] for plane in force]
            piece_ref[slot, half * GROUP : (half + 1) * GROUP, :] = jnp.concatenate(parts, axis=1).astype(
                jnp.bfloat16
            )


def update_kernel(poly, sides, now_ref, prev_ref, first_now_ref, first_prev_ref, z_ref, near_ref, mix_ref, planes_ref, out_ref, *scratch):
    now_vmem, prev_vmem, out_vmem, force_a, force_b, modes_ref, square_ref, arrivals, departures = scratch
    length_x, local_y, depth_z = now_vmem.shape
    chunks = arrivals.shape[1]
    length = length_x // chunks

    def rows_of(chunk):
        return pl.ds(chunk * length, length)

    def fetch(chunk):
        rows = rows_of(chunk)
        return [
            pltpu.make_async_copy(now_ref.at[rows], now_vmem.at[rows], arrivals.at[0, chunk]),
            pltpu.make_async_copy(prev_ref.at[rows], prev_vmem.at[rows], arrivals.at[1, chunk]),
        ]

    pieces = departures.shape[0] // chunks

    def send(piece):
        rows = pl.ds(piece * (length // pieces), length // pieces)
        return pltpu.make_async_copy(out_vmem.at[rows], out_ref.at[rows], departures.at[piece])

    for chunk in range(1, chunks):
        for copy in fetch(chunk):
            copy.start()
    mask = row_mask()[None]
    for half in range(local_y // GROUP):
        cols = slice(half * LANES, (half + 1) * LANES)
        both = jnp.concatenate([z_ref[:, cols], near_ref[:, cols]], axis=1)
        modes_ref[:, cols] = jnp.dot(
            jnp.concatenate([both, both, both], axis=1), mix_ref[...], preferred_element_type=jnp.float32
        )
    scale = math.pi * math.pi / 3.0
    y_index = lax.broadcasted_iota(jnp.int32, (local_y, depth_z), 0) + lax.axis_index("slab") * local_y
    z_index = lax.broadcasted_iota(jnp.int32, (local_y, depth_z), 1)
    y_part = y_index.astype(jnp.float32) * (1.0 / sides[1])
    z_part = z_index.astype(jnp.float32) * (1.0 / sides[2])
    square_ref[...] = scale * (y_part * y_part + z_part * z_part)

    def x_square(x):
        part = x * (1.0 / sides[0])
        return scale * (part * part)

    def exact_gain(theta_sq):
        value = poly[-1] * theta_sq + poly[-2]
        for coefficient in poly[-3::-1]:
            value = value * theta_sq + coefficient
        return value

    groups = length_x // GROUP

    def make_force(group, force_ref):
        row = jnp.minimum(group, groups - 1) * GROUP
        for half in range(local_y // GROUP):
            modes = modes_ref[pl.ds(row, GROUP), half * LANES : (half + 1) * LANES]
            spread = jnp.where(mask, jnp.broadcast_to(modes[:, None, :], (GROUP, GROUP, LANES)), 0.0)
            spread = spread.astype(jnp.bfloat16).reshape(GROUP * GROUP, LANES)
            force = jnp.dot(spread, planes_ref[...], preferred_element_type=jnp.float32)
            force_ref[:, half * GROUP : (half + 1) * GROUP, :] = force.reshape(GROUP, GROUP, depth_z)

    middle = 0.5 * (GROUP - 1)
    reach = middle - 1.0
    begin, after = -middle / reach, (1.0 - middle) / reach

    def advance(group, force_ref, now_vmem, prev_vmem):
        row = group * GROUP
        first = row.astype(jnp.float32)
        nodes = [x_square(first + (middle + offset)) for offset in (-reach, 0.0, reach)]
        x_sq = [x_square(first + float(step)) for step in range(GROUP)]
        for y_at in range(0, local_y, GROUP):
            for z_at in range(0, depth_z, LANES):
                tile = (slice(y_at, y_at + GROUP), slice(z_at, z_at + LANES))
                yz_sq = square_ref[tile]
                low, mid, high = [exact_gain(yz_sq + node) for node in nodes]
                slope = (high - low) * 0.5
                bend = (high + low) * 0.5 - mid
                gain = mid + begin * slope + (begin * begin) * bend
                rise = slope * (1.0 / reach) + bend * (after * after - begin * begin)
                turn = bend * (2.0 / (reach * reach))
                for step in range(GROUP):
                    at = (row + step,) + tile
                    two_cos = 2.0 - (yz_sq + x_sq[step]) * gain
                    value = two_cos * now_vmem[at].astype(jnp.float32) - prev_vmem[at].astype(jnp.float32)
                    out_vmem[at] = (value + gain * force_ref[(step,) + tile]).astype(jnp.bfloat16)
                    gain = gain + rise
                    rise = rise + turn

    make_force(0, force_a)
    pairs = length // (2 * GROUP)

    def compute(chunk, now_rows, prev_rows):
        for index in range(pairs):
            group = (chunk * pairs + index) * 2
            make_force(group + 1, force_b)
            advance(group, force_a, now_rows, prev_rows)
            make_force(group + 2, force_a)
            advance(group + 1, force_b, now_rows, prev_rows)
            if (index + 1) * pieces % pairs == 0:
                send(chunk * pieces + (index + 1) * pieces // pairs - 1).start(priority=1)

    def whole(chunk, carry):
        for copy in fetch(chunk):
            copy.wait()
        compute(chunk, now_vmem, prev_vmem)
        return carry

    compute(jnp.int32(0), first_now_ref, first_prev_ref)
    lax.fori_loop(1, chunks, whole, 0)
    for piece in range(pieces * chunks):
        send(piece).wait()


def planes_kernel(arrived_ref, table_ref, out_ref):
    out = lax.dot_general(
        arrived_ref[...], table_ref[...], (((0,), (0,)), ((), ())), preferred_element_type=jnp.float32
    )
    out_ref[...] = out


def smem():
    return pl.BlockSpec(memory_space=pltpu.SMEM)


def vmem():
    return pl.BlockSpec(memory_space=pltpu.VMEM)


def hbm():
    return pl.BlockSpec(memory_space=pltpu.HBM)


def limit(mib):
    return pltpu.CompilerParams(vmem_limit_bytes=mib << 20)


def shards(modes_now, modes_prev, face_partner):
    slab_count = lax.axis_size("slab")
    _, length_x, local_y, depth_z = modes_now.shape
    length_y = local_y * slab_count
    local_x = length_x // slab_count
    assert local_y % GROUP == 0 and length_x % (4 * GROUP) == 0
    count = local_y // GROUP
    bf = jnp.bfloat16
    current = pltpu.with_memory_space_constraint(modes_now[0], pltpu.HBM)
    earlier = pltpu.with_memory_space_constraint(modes_prev[0], pltpu.HBM)
    planes = jnp.asarray(np.ascontiguousarray(spread_columns(depth_z).T))
    mix = jnp.asarray(force_matrix())
    table_x = jnp.asarray(cosine_table(length_x).astype(bf16))
    table_y = jnp.asarray(cosine_table(length_y).astype(bf16))

    chunks = 8
    first_rows = jax.ShapeDtypeStruct((length_x // chunks, local_y, depth_z), bf)
    z_own, pack, first_now, first_prev = pl.pallas_call(
        sections_kernel,
        in_specs=[hbm()] * 2,
        out_specs=[vmem()] * 4,
        out_shape=[
            jax.ShapeDtypeStruct((length_x, count * LANES), bf),
            jax.ShapeDtypeStruct((count * length_x // 4, 3 * LANES), bf),
            first_rows,
            first_rows,
        ],
        scratch_shapes=[
            pltpu.VMEM((length_x, local_y, depth_z), bf),
            pltpu.SemaphoreType.DMA((SECTION_CHUNKS,)),
            pltpu.SemaphoreType.DMA((2,)),
        ],
        compiler_params=limit(16),
        name="sections",
    )(current, earlier)

    rect_count = lax.axis_size("rect")
    if rect_count in DIRECT:
        every = [pack]
        for distance in range(1, rect_count):
            pairs = [(j, j ^ distance) for j in range(rect_count)]
            every.append(lax.ppermute(pack, "rect", pairs))
    else:
        every = [lax.all_gather(pack, "rect", axis=0)]
    near, pieces = pl.pallas_call(
        forces_kernel,
        in_specs=[smem()] + [vmem()] * (2 + len(every)),
        out_specs=[vmem()] * 2,
        out_shape=[
            jax.ShapeDtypeStruct((length_x, count * LANES), bf),
            jax.ShapeDtypeStruct((slab_count, local_y, PLANES * local_x), bf),
        ],
        compiler_params=limit(8),
        name="forces",
    )(face_partner, z_own, *every, table_x)

    arrived = lax.all_to_all(pieces, "slab", split_axis=0, concat_axis=0, tiled=True)

    wide = (length_x, local_y, depth_z)
    fresh = pl.pallas_call(
        functools.partial(update_kernel, gain_polynomial(5), (length_x, length_y, depth_z)),
        in_specs=[hbm(), hbm()] + [vmem()] * 6,
        out_specs=hbm(),
        out_shape=jax.ShapeDtypeStruct(wide, bf),
        scratch_shapes=[
            *[pltpu.VMEM(wide, bf)] * 3,
            *[pltpu.VMEM((GROUP, local_y, depth_z), jnp.float32)] * 2,
            pltpu.VMEM((length_x, count * LANES), jnp.float32),
            pltpu.VMEM((local_y, depth_z), jnp.float32),
            pltpu.SemaphoreType.DMA((2, chunks)),
            pltpu.SemaphoreType.DMA((2 * chunks,)),
        ],
        compiler_params=limit(40),
        name="update",
    )(current, earlier, first_now, first_prev, z_own, near, mix, planes)

    forcing = pl.pallas_call(
        planes_kernel,
        in_specs=[vmem()] * 2,
        out_specs=vmem(),
        out_shape=jax.ShapeDtypeStruct((PLANES * local_x, length_y), jnp.float32),
        compiler_params=limit(8),
        name="planes",
    )(arrived.reshape(length_y, PLANES * local_x), table_y)
    return (fresh[None], forcing.reshape(1, PLANES, local_x, length_y))


def solution(mesh):
    return jax.shard_map(
        shards,
        mesh=mesh,
        in_specs=(P("rect", None, "slab", None), P("rect", None, "slab", None), P()),
        out_specs=(P("rect", None, "slab", None), P("rect", None, "slab", None)),
        check_vma=False,
    )
```

```python
import functools
import math

import jax
import jax.numpy as jnp
import ml_dtypes
import numpy as np
from jax import lax
from jax.experimental import pallas as pl
from jax.experimental.pallas import tpu as pltpu
from jax.sharding import PartitionSpec as P

courant_sq = 1.0 / 3.0
coeffs = (1.5, -0.15, 2.0 / 180.0)
bf16 = ml_dtypes.bfloat16
PLANES = 6
LANES = 128
GROUP = 16
USED = PLANES * GROUP
SECTION_CHUNKS = 4
DIRECT = ()


def cosine_table(length):
    mode_index = np.arange(length, dtype=np.int64)[:, None]
    cell_index = np.arange(length, dtype=np.int64)[None, :]
    phase = mode_index * (2 * cell_index + 1) % (4 * length)
    angles = phase.astype(np.float32) * np.float32(math.pi / (2.0 * length))
    weights = np.where(mode_index == 0, math.sqrt(1.0 / length), math.sqrt(2.0 / length))
    return weights.astype(np.float32) * np.cos(angles)


def plane_columns(depth_z):
    table = cosine_table(depth_z)
    return np.concatenate([table[:, :3], table[:, depth_z - 3 :]], axis=1).astype(bf16)


def spread_columns(depth_z):
    columns = plane_columns(depth_z)
    out = np.zeros((depth_z, LANES), bf16)
    out[:, :USED] = np.repeat(columns, GROUP, axis=1)
    return out


def section_columns(depth_z):
    mode = lax.broadcasted_iota(jnp.int32, (depth_z, LANES), 0)
    lane = lax.broadcasted_iota(jnp.int32, (depth_z, LANES), 1)
    plane = lane // GROUP
    cell = jnp.where(plane < 3, plane, depth_z - PLANES + plane)
    phase = mode * (2 * cell + 1) % (4 * depth_z)
    angle = phase.astype(jnp.float32) * (math.pi / (2.0 * depth_z))
    weight = jnp.where(mode == 0, math.sqrt(1.0 / depth_z), math.sqrt(2.0 / depth_z))
    return jnp.where(lane < USED, weight * jnp.cos(angle), 0.0).astype(jnp.bfloat16)


def force_matrix():
    own = np.zeros((PLANES, PLANES), np.float64)
    other = np.zeros((PLANES, PLANES), np.float64)
    for m in range(3):
        for k in range(3 - m):
            weight = courant_sq * coeffs[m + k]
            other[5 - k, m] += weight
            own[k, m] -= weight
            other[k, 5 - m] += weight
            own[5 - k, 5 - m] -= weight
    full = np.zeros((2 * LANES, LANES), np.float64)
    for row in range(GROUP):
        full[row:USED:GROUP, row:USED:GROUP] = own
        full[LANES + row : LANES + USED : GROUP, row:USED:GROUP] = other
    terms = []
    rest = full
    for _ in range(3):
        term = rest.astype(np.float32).astype(bf16)
        terms.append(term)
        rest = rest - term.astype(np.float64)
    return np.concatenate(terms, axis=0)


def gain_polynomial(degree):
    top = math.pi * math.pi

    def exact(t):
        t = np.asarray(t, np.float64)
        theta = np.sqrt(np.maximum(t, 1e-12))
        return np.where(t > 1e-10, (2.0 * np.sin(0.5 * theta) / theta) ** 2, 1.0)

    fit = np.polynomial.chebyshev.Chebyshev.interpolate(exact, degree, domain=[0.0, top * 1.0001])
    return [float(c) for c in fit.convert(kind=np.polynomial.Polynomial, domain=[-1, 1]).coef]


def row_mask():
    rows = lax.broadcasted_iota(jnp.int32, (GROUP, LANES), 0)
    lanes = lax.broadcasted_iota(jnp.int32, (GROUP, LANES), 1)
    return (lanes % GROUP == rows) & (lanes < USED)


def packed_lower_mask(shape):
    lanes = lax.broadcasted_iota(jnp.int32, shape, len(shape) - 1)
    tile = lanes // LANES
    inner = lanes % LANES
    plane = jnp.where(inner < USED, inner // GROUP, 2 * tile + (inner - USED) // GROUP)
    return plane < 3


def gather_rows(section, row_of_lane, sublane):
    values = jnp.where((row_of_lane < 8)[None], section[:, :8], section[:, 8:])
    for distance in (4, 2, 1):
        count = values.shape[0] // 2
        first, second = values[:count], values[count:]
        early = ((sublane & distance) == 0)[None]
        late_row = ((row_of_lane & distance) != 0)[None]
        if distance == 4:
            kept = jnp.where(early, first, second)
            moved = pltpu.roll(jnp.where(early, second, first), 4, 1)
            values = jnp.where(early != late_row, kept, moved)
        else:
            up = pltpu.roll(first, 8 - distance, 1)
            down = pltpu.roll(second, distance, 1)
            values = jnp.where(early, jnp.where(late_row, up, first), jnp.where(late_row, second, down))
    return values[0]


def sections_kernel(now_ref, prev_ref, z_ref, pack_ref, first_now_ref, first_prev_ref, now_vmem, arrivals, extras):
    count = now_ref.shape[1] // GROUP
    packed_rows = now_ref.shape[0] // 4
    chunks = arrivals.shape[0]
    length = now_ref.shape[0] // chunks

    def fetch(chunk):
        rows = pl.ds(chunk * length, length)
        return pltpu.make_async_copy(now_ref.at[rows], now_vmem.at[rows], arrivals.at[chunk])

    for chunk in range(chunks):
        fetch(chunk).start()
    first = pl.ds(0, first_now_ref.shape[0])
    keeps = [
        pltpu.make_async_copy(now_ref.at[first], first_now_ref, extras.at[0]),
        pltpu.make_async_copy(prev_ref.at[first], first_prev_ref, extras.at[1]),
    ]
    for copy in keeps:
        copy.start()
    columns = section_columns(now_ref.shape[2])
    sublane = lax.broadcasted_iota(jnp.int32, (8, LANES), 0)
    row_of_lane = lax.broadcasted_iota(jnp.int32, (8, LANES), 1) % GROUP
    lane = lax.broadcasted_iota(jnp.int32, (GROUP, LANES), 1)

    def step_rows(step):
        halves = [[] for _ in range(count)]
        for part in range(4):
            rows = pl.ds((step * 4 + part) * GROUP, GROUP)
            flat = now_vmem[rows].reshape(GROUP * now_vmem.shape[1], now_vmem.shape[2])
            section = jnp.dot(flat, columns, preferred_element_type=jnp.float32)
            section = section.reshape(GROUP, count, GROUP, LANES)
            for half in range(count):
                picked = jnp.concatenate(
                    [gather_rows(section[i : i + 8, half], row_of_lane, sublane) for i in range(0, GROUP, 8)], axis=0
                ).astype(jnp.bfloat16)
                z_ref[rows, half * LANES : (half + 1) * LANES] = picked
                halves[half].append(picked.astype(jnp.float32))
        for half in range(count):
            for tile in range(3):
                moved = pltpu.roll(halves[half][3], USED - 32 * tile, 1)
                pack_ref[pl.ds(half * packed_rows + step * GROUP, GROUP), tile * LANES : (tile + 1) * LANES] = jnp.where(
                    lane < USED, halves[half][tile], moved
                ).astype(jnp.bfloat16)

    steps = length // (4 * GROUP)

    def body(chunk, carry):
        fetch(chunk).wait()
        for step in range(steps):
            step_rows(chunk * steps + step)
        return carry

    lax.fori_loop(0, chunks, body, 0)
    for copy in keeps:
        copy.wait()


def neighbours(face_ref, rect):
    partner = face_ref[rect]
    source = jnp.int32(0)
    for index in range(face_ref.shape[0]):
        source = source + jnp.where(face_ref[index] == rect, jnp.int32(index), jnp.int32(0))
    return partner, source


def forces_kernel(face_ref, z_ref, *refs):
    *every_refs, table_ref, near_ref, piece_out_ref, piece_ref, departures = refs
    count = z_ref.shape[1] // LANES
    rect = lax.axis_index("rect")
    partner, source = neighbours(face_ref, rect)
    packed_rows = every_refs[0].shape[-2] // count
    lower = packed_lower_mask((packed_rows, every_refs[0].shape[-1]))

    def pack_of(other, rows):
        if len(every_refs) == 1:
            return every_refs[0][other, rows].astype(jnp.float32)
        value = every_refs[0][rows].astype(jnp.float32)
        for distance, ref in enumerate(every_refs[1:], 1):
            value = jnp.where(other == (rect ^ distance), ref[rows].astype(jnp.float32), value)
        return value

    blocks = packed_rows // GROUP
    lane = lax.broadcasted_iota(jnp.int32, (blocks, GROUP, LANES), 2)
    for half in range(count):
        rows = pl.ds(half * packed_rows, packed_rows)
        packed = jnp.where(lower, pack_of(partner, rows), pack_of(source, rows))
        tiles = [
            packed[:, tile * LANES : (tile + 1) * LANES].reshape(blocks, GROUP, LANES) for tile in range(3)
        ]
        moved = [
            pltpu.roll(packed[:, tile * LANES : (tile + 1) * LANES], 32 * (tile + 1), 1).reshape(
                blocks, GROUP, LANES
            )
            for tile in range(3)
        ]
        last = jnp.where(lane < 32, moved[0], jnp.where(lane < 64, moved[1], moved[2]))
        for group, value in enumerate(tiles + [last]):
            value = jnp.where(lane < USED, value, 0.0).astype(jnp.bfloat16)
            for block in range(blocks):
                start = (block * 4 + group) * GROUP
                near_ref[start : start + GROUP, half * LANES : (half + 1) * LANES] = value[block]
    modes = jnp.concatenate([z_ref[...], near_ref[...]], axis=1)
    cells = lax.dot_general(
        modes, table_ref[...], (((0,), (0,)), ((), ())), preferred_element_type=jnp.float32
    )
    cells = cells.astype(jnp.bfloat16).astype(jnp.float32)

    def sections_of(tile):
        return [cells[tile * LANES + p * GROUP : tile * LANES + (p + 1) * GROUP] for p in range(PLANES)]

    copies = []
    for half in range(count):
        own = sections_of(half)
        near = sections_of(count + half)
        jump_up = [near[k] - own[5 - k] for k in range(3)]
        jump_down = [near[5 - k] - own[k] for k in range(3)]
        force = [None] * PLANES
        for m in range(3):
            down = coeffs[m] * jump_down[0]
            up = coeffs[m] * jump_up[0]
            for k in range(1, 3 - m):
                down = down + coeffs[m + k] * jump_down[k]
                up = up + coeffs[m + k] * jump_up[k]
            force[m] = courant_sq * down
            force[5 - m] = courant_sq * up
        width = piece_ref.shape[2] // PLANES
        for slot in range(piece_ref.shape[0]):
            parts = [plane[:, slot * width : (slot + 1) * width] for plane in force]
            piece_ref[slot, half * GROUP : (half + 1) * GROUP, :] = jnp.concatenate(parts, axis=1).astype(
                jnp.bfloat16
            )
        rows = slice(half * GROUP, (half + 1) * GROUP)
        copies.append(
            pltpu.make_async_copy(piece_ref.at[:, rows], piece_out_ref.at[:, rows], departures.at[half])
        )
        copies[-1].start()
    for copy in copies:
        copy.wait()


def update_kernel(poly, sides, now_ref, prev_ref, first_now_ref, first_prev_ref, z_ref, near_ref, mix_ref, planes_ref, out_ref, *scratch):
    now_vmem, prev_vmem, out_vmem, force_a, force_b, modes_ref, square_ref, arrivals, departures = scratch
    length_x, local_y, depth_z = now_vmem.shape
    chunks = arrivals.shape[1]
    length = length_x // chunks

    def rows_of(chunk):
        return pl.ds(chunk * length, length)

    def fetch(chunk):
        rows = rows_of(chunk)
        return [
            pltpu.make_async_copy(now_ref.at[rows], now_vmem.at[rows], arrivals.at[0, chunk]),
            pltpu.make_async_copy(prev_ref.at[rows], prev_vmem.at[rows], arrivals.at[1, chunk]),
        ]

    pieces = departures.shape[0] // chunks

    def send(piece):
        rows = pl.ds(piece * (length // pieces), length // pieces)
        return pltpu.make_async_copy(out_vmem.at[rows], out_ref.at[rows], departures.at[piece])

    for chunk in range(1, chunks):
        for copy in fetch(chunk):
            copy.start()
    mask = row_mask()[None]
    for half in range(local_y // GROUP):
        cols = slice(half * LANES, (half + 1) * LANES)
        both = jnp.concatenate([z_ref[:, cols], near_ref[:, cols]], axis=1)
        modes_ref[:, cols] = jnp.dot(
            jnp.concatenate([both, both, both], axis=1), mix_ref[...], preferred_element_type=jnp.float32
        )
    scale = math.pi * math.pi / 3.0
    y_index = lax.broadcasted_iota(jnp.int32, (local_y, depth_z), 0) + lax.axis_index("slab") * local_y
    z_index = lax.broadcasted_iota(jnp.int32, (local_y, depth_z), 1)
    y_part = y_index.astype(jnp.float32) * (1.0 / sides[1])
    z_part = z_index.astype(jnp.float32) * (1.0 / sides[2])
    square_ref[...] = scale * (y_part * y_part + z_part * z_part)

    def x_square(x):
        part = x * (1.0 / sides[0])
        return scale * (part * part)

    def exact_gain(theta_sq):
        value = poly[-1] * theta_sq + poly[-2]
        for coefficient in poly[-3::-1]:
            value = value * theta_sq + coefficient
        return value

    groups = length_x // GROUP

    def make_force(group, force_ref):
        row = jnp.minimum(group, groups - 1) * GROUP
        for half in range(local_y // GROUP):
            modes = modes_ref[pl.ds(row, GROUP), half * LANES : (half + 1) * LANES]
            spread = jnp.where(mask, jnp.broadcast_to(modes[:, None, :], (GROUP, GROUP, LANES)), 0.0)
            spread = spread.astype(jnp.bfloat16).reshape(GROUP * GROUP, LANES)
            force = jnp.dot(spread, planes_ref[...], preferred_element_type=jnp.float32)
            force_ref[:, half * GROUP : (half + 1) * GROUP, :] = force.reshape(GROUP, GROUP, depth_z)

    middle = 0.5 * (GROUP - 1)
    reach = middle - 1.0
    begin, after = -middle / reach, (1.0 - middle) / reach

    def advance(group, force_ref, now_vmem, prev_vmem):
        row = group * GROUP
        first = row.astype(jnp.float32)
        nodes = [x_square(first + (middle + offset)) for offset in (-reach, 0.0, reach)]
        x_sq = [x_square(first + float(step)) for step in range(GROUP)]
        for y_at in range(0, local_y, GROUP):
            for z_at in range(0, depth_z, LANES):
                tile = (slice(y_at, y_at + GROUP), slice(z_at, z_at + LANES))
                yz_sq = square_ref[tile]
                low, mid, high = [exact_gain(yz_sq + node) for node in nodes]
                slope = (high - low) * 0.5
                bend = (high + low) * 0.5 - mid
                gain = mid + begin * slope + (begin * begin) * bend
                rise = slope * (1.0 / reach) + bend * (after * after - begin * begin)
                turn = bend * (2.0 / (reach * reach))
                for step in range(GROUP):
                    at = (row + step,) + tile
                    two_cos = 2.0 - (yz_sq + x_sq[step]) * gain
                    value = two_cos * now_vmem[at].astype(jnp.float32) - prev_vmem[at].astype(jnp.float32)
                    out_vmem[at] = (value + gain * force_ref[(step,) + tile]).astype(jnp.bfloat16)
                    gain = gain + rise
                    rise = rise + turn

    make_force(0, force_a)
    pairs = length // (2 * GROUP)

    def compute(chunk, now_rows, prev_rows):
        for index in range(pairs):
            group = (chunk * pairs + index) * 2
            make_force(group + 1, force_b)
            advance(group, force_a, now_rows, prev_rows)
            make_force(group + 2, force_a)
            advance(group + 1, force_b, now_rows, prev_rows)
            if (index + 1) * pieces % pairs == 0:
                send(chunk * pieces + (index + 1) * pieces // pairs - 1).start(priority=1)

    def whole(chunk, carry):
        for copy in fetch(chunk):
            copy.wait()
        compute(chunk, now_vmem, prev_vmem)
        return carry

    compute(jnp.int32(0), first_now_ref, first_prev_ref)
    lax.fori_loop(1, chunks, whole, 0)
    for piece in range(pieces * chunks):
        send(piece).wait()


def planes_kernel(arrived_ref, table_ref, out_ref, out_vmem, departures):
    parts = departures.shape[0]
    length = out_vmem.shape[0] // parts
    copies = []
    for part in range(parts):
        rows = slice(part * length, (part + 1) * length)
        out_vmem[rows] = lax.dot_general(
            arrived_ref[:, rows], table_ref[...], (((0,), (0,)), ((), ())), preferred_element_type=jnp.float32
        )
        copies.append(pltpu.make_async_copy(out_vmem.at[rows], out_ref.at[rows], departures.at[part]))
        copies[-1].start()
    for copy in copies:
        copy.wait()


def smem():
    return pl.BlockSpec(memory_space=pltpu.SMEM)


def vmem():
    return pl.BlockSpec(memory_space=pltpu.VMEM)


def hbm():
    return pl.BlockSpec(memory_space=pltpu.HBM)


def limit(mib):
    return pltpu.CompilerParams(vmem_limit_bytes=mib << 20)


def shards(modes_now, modes_prev, face_partner):
    slab_count = lax.axis_size("slab")
    _, length_x, local_y, depth_z = modes_now.shape
    length_y = local_y * slab_count
    local_x = length_x // slab_count
    assert local_y % GROUP == 0 and length_x % (4 * GROUP) == 0
    count = local_y // GROUP
    bf = jnp.bfloat16
    current = pltpu.with_memory_space_constraint(modes_now[0], pltpu.HBM)
    earlier = pltpu.with_memory_space_constraint(modes_prev[0], pltpu.HBM)
    planes = jnp.asarray(np.ascontiguousarray(spread_columns(depth_z).T))
    mix = jnp.asarray(force_matrix())
    table_x = jnp.asarray(cosine_table(length_x).astype(bf16))
    table_y = jnp.asarray(cosine_table(length_y).astype(bf16))

    chunks = 8
    first_rows = jax.ShapeDtypeStruct((length_x // chunks, local_y, depth_z), bf)
    z_own, pack, first_now, first_prev = pl.pallas_call(
        sections_kernel,
        in_specs=[hbm()] * 2,
        out_specs=[vmem()] * 4,
        out_shape=[
            jax.ShapeDtypeStruct((length_x, count * LANES), bf),
            jax.ShapeDtypeStruct((count * length_x // 4, 3 * LANES), bf),
            first_rows,
            first_rows,
        ],
        scratch_shapes=[
            pltpu.VMEM((length_x, local_y, depth_z), bf),
            pltpu.SemaphoreType.DMA((SECTION_CHUNKS,)),
            pltpu.SemaphoreType.DMA((2,)),
        ],
        compiler_params=limit(16),
        name="sections",
    )(current, earlier)

    rect_count = lax.axis_size("rect")
    if rect_count in DIRECT:
        every = [pack]
        for distance in range(1, rect_count):
            pairs = [(j, j ^ distance) for j in range(rect_count)]
            every.append(lax.ppermute(pack, "rect", pairs))
    else:
        every = [lax.all_gather(pack, "rect", axis=0)]
    piece_shape = (slab_count, local_y, PLANES * local_x)
    near, pieces = pl.pallas_call(
        forces_kernel,
        in_specs=[smem()] + [vmem()] * (2 + len(every)),
        out_specs=[vmem(), hbm()],
        out_shape=[
            jax.ShapeDtypeStruct((length_x, count * LANES), bf),
            jax.ShapeDtypeStruct(piece_shape, bf),
        ],
        scratch_shapes=[pltpu.VMEM(piece_shape, bf), pltpu.SemaphoreType.DMA((count,))],
        compiler_params=limit(8),
        name="forces",
    )(face_partner, z_own, *every, table_x)

    arrived = lax.all_to_all(pieces, "slab", split_axis=0, concat_axis=0, tiled=True)

    wide = (length_x, local_y, depth_z)
    fresh = pl.pallas_call(
        functools.partial(update_kernel, gain_polynomial(5), (length_x, length_y, depth_z)),
        in_specs=[hbm(), hbm()] + [vmem()] * 6,
        out_specs=hbm(),
        out_shape=jax.ShapeDtypeStruct(wide, bf),
        scratch_shapes=[
            *[pltpu.VMEM(wide, bf)] * 3,
            *[pltpu.VMEM((GROUP, local_y, depth_z), jnp.float32)] * 2,
            pltpu.VMEM((length_x, count * LANES), jnp.float32),
            pltpu.VMEM((local_y, depth_z), jnp.float32),
            pltpu.SemaphoreType.DMA((2, chunks)),
            pltpu.SemaphoreType.DMA((2 * chunks,)),
        ],
        compiler_params=limit(40),
        name="update",
    )(current, earlier, first_now, first_prev, z_own, near, mix, planes)

    cells = (PLANES * local_x, length_y)
    forcing = pl.pallas_call(
        planes_kernel,
        in_specs=[vmem()] * 2,
        out_specs=hbm(),
        out_shape=jax.ShapeDtypeStruct(cells, jnp.float32),
        scratch_shapes=[pltpu.VMEM(cells, jnp.float32), pltpu.SemaphoreType.DMA((3,))],
        compiler_params=limit(8),
        name="planes",
    )(arrived.reshape(length_y, PLANES * local_x), table_y)
    return (fresh[None], forcing.reshape(1, PLANES, local_x, length_y))


def solution(mesh):
    return jax.shard_map(
        shards,
        mesh=mesh,
        in_specs=(P("rect", None, "slab", None), P("rect", None, "slab", None), P()),
        out_specs=(P("rect", None, "slab", None), P("rect", None, "slab", None)),
        check_vma=False,
    )
```
